512 devices in a mesh: chan: 32 (over x, z), tm: 16 (over y, core).
Axes of the slice: x: 4, y: 8, z: 8, core: 2. Of those that a mesh axis runs over, the one named last changes fastest.
Arguments:
- samples: bfloat16 [8192, 65536], P('chan', 'tm'), may hold values from -40 to 40, as said below
- start_chan: float32 [8192, 64], P('chan'), may hold values from 0.1 to 1
- start_freq: float32 [512, 64], replicated, may hold values from 0.1 to 1
- start_time: float32 [128, 64], P('tm'), may hold values from 0.1 to 1
Outputs:
- factor_chan: float32 [8192, 64], P('chan')
- factor_freq: float32 [512, 64], replicated
- factor_time: float32 [128, 64], P('tm')
The draws below stay inside these ranges and needn't reach their ends.
Inputs may be any that keep to these rules, and one draw needn't show every extreme that they name: `samples`: channel amplitudes differ from channel to channel and along the fibre; values lie within the stated bounds.
All inputs are finite; a program needn't handle non-finite values.
Results may differ from the reference program's by a relative error of at most 0.003.
Values may be sent and summed in bfloat16 or wider, within the bound.
No kernel may reach another device: no remote copies, remote signals or barrier semaphores. Data moves between devices by JAX's collectives and lax.ppermute only.
A program may use at most 64 MiB of HBM per device.

```python
import jax
import jax.numpy as jnp
from jax import lax

C_DEV = 256
FRAME = 1024
HOP = 512
BINS = 512
RANK = 64
ITERS = 5
CHANNELS = 8192
FRAMES = 128
SAMPLES = 65536
N_CHAN = 32


def draw_samples(key, part):
    key_noise, key_row, key_col = jax.random.split(key, 3)
    position = jnp.arange(CHANNELS, dtype=jnp.float32) / CHANNELS
    row_scale = 10.0 ** (0.5 * jax.random.uniform(key_row, (CHANNELS,), jnp.float32))
    row_scale = row_scale * 3.0 ** (-0.5 * position)
    col_scale = 10.0 ** (0.5 * jax.random.uniform(key_col, (SAMPLES,), jnp.float32))
    noise = jnp.clip(jax.random.normal(key_noise, (CHANNELS, SAMPLES), jnp.float32), -4.0, 4.0)
    values = noise * row_scale[:, None] * col_scale[None, :]
    return jnp.clip(values, -40.0, 40.0).astype(jnp.bfloat16)


def shard_levels(key, shape, cuts, least, largest):
    loudness = 1.0
    for axis_at, parts in cuts:
        draws = jax.random.uniform(jax.random.fold_in(jax.random.fold_in(key, 6), axis_at), (parts,), jnp.float32, least / len(cuts), largest / len(cuts))
        loudness = loudness * jnp.repeat(jnp.exp(draws), shape[axis_at] // parts).reshape((-1,) + (1,) * (len(shape) - 1 - axis_at))
    return loudness


def setup_inputs(seed: int = 0) -> dict:
    splits = jax.random.split(jax.random.key(seed), 5)
    samples = draw_samples(jax.random.fold_in(splits[4], 71), 0)
    start_chan = jnp.clip(0.1 + 0.9 * jax.random.uniform(splits[1], (CHANNELS, RANK), jnp.float32) ** shard_levels(splits[1], (CHANNELS, RANK), ((0, 32),), -0.2, 0.2), 0.1, 1.0)
    start_freq = jnp.clip(jax.random.uniform(splits[2], (BINS, RANK), jnp.float32, 0.1, 1.0), 0.1, 1.0)
    start_time = jnp.clip(0.1 + 0.9 * jax.random.uniform(splits[3], (FRAMES, RANK), jnp.float32) ** shard_levels(splits[3], (FRAMES, RANK), ((0, 16),), -0.2, 0.2), 0.1, 1.0)
    return dict(samples=samples, start_chan=start_chan, start_freq=start_freq, start_time=start_time)


def make_table(frame_len):
    half = frame_len // 2
    index_n = jnp.arange(frame_len, dtype=jnp.int32)
    index_k = jnp.arange(half, dtype=jnp.int32)
    phase = (index_n[:, None] * index_k[None, :] % frame_len).astype(jnp.float32)
    angle = 2.0 * jnp.pi * phase / frame_len
    window = 0.5 - 0.5 * jnp.cos(2.0 * jnp.pi * index_n.astype(jnp.float32) / frame_len)
    cosine = window[:, None] * jnp.cos(angle)
    sine = -window[:, None] * jnp.sin(angle)
    return jnp.concatenate([cosine, sine], axis=1).astype(jnp.bfloat16)

def admm_sweep(product, previous, gram):
    rank_size = gram.shape[0]
    penalty = jnp.trace(gram) / rank_size
    identity = jnp.eye(rank_size, dtype=gram.dtype)
    lower = jnp.linalg.cholesky(gram + penalty * identity)
    inverse = jax.scipy.linalg.cho_solve((lower, True), identity)
    current = previous
    dual_var = jnp.zeros_like(previous)
    for step in range(ITERS):
        target = jnp.dot(product + penalty * (current + dual_var), inverse, precision=lax.Precision.HIGHEST)
        current = jnp.maximum(target - dual_var, 0.0)
        dual_var = dual_var + current - target
    return current

def reference(samples, start_chan, start_freq, start_time):
    dft_table = make_table(FRAME).astype(jnp.float32)
    blocks_in = samples.reshape(N_CHAN, C_DEV, SAMPLES)

    def one_block(block):
        padded = jnp.concatenate([block, jnp.zeros((block.shape[0], HOP), block.dtype)], axis=1)
        pieces = padded.reshape(block.shape[0], FRAMES + 1, HOP)
        frames = jnp.concatenate([pieces[:, :-1], pieces[:, 1:]], axis=2).reshape(-1, FRAME)
        spectrum = jnp.dot(frames.astype(jnp.float32), dft_table, precision=lax.Precision.HIGHEST)
        power_spec = (spectrum[:, :BINS] ** 2 + spectrum[:, BINS:] ** 2) / (3.0 * FRAME / 8.0)
        return power_spec.reshape(block.shape[0], FRAMES, BINS)
    spec = lax.map(one_block, blocks_in).reshape(CHANNELS, FRAMES, BINS)
    high = lax.Precision.HIGHEST
    gram_time = jnp.dot(start_time.T, start_time, precision=high)
    gram_freq = jnp.dot(start_freq.T, start_freq, precision=high)
    mixed = jnp.einsum('ctf,fr->ctr', spec, start_freq, precision=high)
    m_chan = jnp.sum(mixed * start_time[None], axis=1)
    factor_chan = admm_sweep(m_chan, start_chan, gram_freq * gram_time)
    gram_chan = jnp.dot(factor_chan.T, factor_chan, precision=high)
    weights = factor_chan[:, None, :] * start_time[None]
    m_freq = jnp.einsum('ctf,ctr->fr', spec, weights, precision=high)
    factor_freq = admm_sweep(m_freq, start_freq, gram_chan * gram_time)
    mixed_two = jnp.einsum('ctf,fr->ctr', spec, factor_freq, precision=high)
    m_time = jnp.einsum('ctr,cr->tr', mixed_two, factor_chan, precision=high)
    gram_new = jnp.dot(factor_freq.T, factor_freq, precision=high)
    factor_time = admm_sweep(m_time, start_time, gram_chan * gram_new)
    return (factor_chan, factor_freq, factor_time)
```

```python
import numpy as np
import jax
import jax.numpy as jnp
from jax import lax
from jax.experimental import pallas as pl
from jax.experimental.pallas import tpu as pltpu
from jax.sharding import Mesh
from jax.sharding import PartitionSpec as P

FRAME = 1024
HALF = FRAME // 2
BINS = 512
RANK = 64
ITERS = 5
FRAMES_HERE = 8
CHANS_HERE = 256
PACK = 2 * RANK
TM = ("tm_0", "tm_1")
N_TM = 16
N_X = 4
N_Z = 8
SCALE = 1.0 / (3.0 * FRAME / 8.0)
F32 = jnp.float32
BF16 = jnp.bfloat16
HIGH = lax.Precision.HIGHEST


def half_tables():
    n = np.arange(HALF)[None, :]
    j = np.arange(BINS // 2)[:, None]
    even = 2.0 * np.pi * ((n * (2 * j)) % FRAME) / FRAME
    odd = 2.0 * np.pi * ((n * (2 * j + 1)) % FRAME) / FRAME
    stack = lambda a: np.concatenate([np.cos(a), np.sin(a)], axis=0)
    return stack(even).astype(BF16), stack(odd).astype(BF16)


def window_row():
    n = np.arange(HALF)[None, :]
    return (0.5 - 0.5 * np.cos(2.0 * np.pi * n / FRAME)).astype(np.float32)


def lane_is_low(shape):
    return lax.broadcasted_iota(jnp.int32, shape, 1) < RANK


def both_halves(x):
    other = pltpu.roll(x, RANK, 1)
    low = lane_is_low(x.shape)
    return jnp.concatenate([jnp.where(low, x, other), jnp.where(low, other, x)], axis=0)


def side_by_side(x):
    m = x.shape[0] // 2
    return jnp.where(lane_is_low((m, PACK)), x[:m], x[m:])


def high_low(x):
    high = x.astype(BF16).astype(F32)
    return jnp.where(lane_is_low(x.shape), high, x - high).astype(BF16)


def doubled(x):
    return jnp.concatenate([x, x], axis=1)


def gram_of(x):
    return lax.dot_general(x, x, (((0,), (0,)), ((), ())), precision=HIGH,
                           preferred_element_type=F32)


def inverse_of(gram):
    row = lax.broadcasted_iota(jnp.int32, gram.shape, 0)
    col = lax.broadcasted_iota(jnp.int32, gram.shape, 1)
    eye = jnp.where(row == col, 1.0, 0.0).astype(F32)
    penalty = jnp.sum(gram * eye) / PACK
    block = (row < RANK) == (col < RANK)
    a = jnp.where(block, gram * (1.0 / penalty), 0.0) + eye
    spread = (RANK / 2.0) / (RANK / 2.0 + 1.0)
    mid = RANK / 2.0 + 1.0
    centre = 1.0 - spread * spread / 2.0
    x = (eye * (2.0 / mid) - a * (1.0 / (mid * mid))) * (1.0 / centre)
    spread = (spread * spread / 2.0) / centre
    for _ in range(5):
        s = jnp.dot(a, x, precision=HIGH, preferred_element_type=F32)
        centre = 1.0 - spread * spread / 2.0
        x = jnp.dot(x, (2.0 * eye - s) * (1.0 / centre), precision=HIGH,
                    preferred_element_type=F32)
        spread = (spread * spread / 2.0) / centre
    return penalty, x


def admm(product, previous, penalty, inverse):
    scaled = product * (1.0 / penalty)
    carried = previous
    dual = jnp.zeros_like(previous)
    value = previous
    for _ in range(ITERS):
        target = jnp.dot(scaled + carried, inverse, precision=HIGH, preferred_element_type=F32)
        value = target - dual
        dual = jnp.maximum(-value, 0.0)
        carried = jnp.abs(value)
    return jnp.maximum(value, 0.0)


def prep_kernel(freq_ref, time_ref, packed_ref, gram_ref, rows_ref, time2_ref):
    half = BINS // 2
    even = freq_ref[pl.ds(0, half, stride=2), :]
    odd = freq_ref[pl.ds(1, half, stride=2), :]
    packed_ref[...] = jnp.concatenate([even, odd], axis=1)
    twice = jnp.concatenate([doubled(even), doubled(odd)], axis=0)
    gram_ref[...] = gram_of(twice)
    rows_ref[...] = high_low(twice).astype(F32).T.astype(BF16)
    time2_ref[...] = doubled(time_ref[...])


def frame_power(first, second, window, even_ref, odd_ref):
    first = first.astype(F32) * window
    second = second.astype(F32)
    second = second - second * window
    total = (first + second).astype(BF16)
    change = (first - second).astype(BF16)
    dims = (((1,), (1,)), ((), ()))
    half = BINS // 2
    out = []
    for table, side in ((even_ref, total), (odd_ref, change)):
        wave = lax.dot_general(table[...], side, dims, preferred_element_type=F32)
        out.append((wave[:half] * wave[:half] + wave[half:] * wave[half:]).astype(BF16))
    return jnp.concatenate(out, axis=0)


def chan_term(rows_ref, power, time_row):
    q = jnp.dot(rows_ref[...], power, preferred_element_type=F32)
    row = lax.broadcasted_iota(jnp.int32, (PACK, PACK), 0)
    col = lax.broadcasted_iota(jnp.int32, (PACK, PACK), 1)
    column = jnp.sum(jnp.where(row == col, time_row, 0.0), axis=1, keepdims=True)
    return q * column


def early_kernel(first_ref, second_ref, window_ref, even_ref, odd_ref, rows_ref, time2_ref,
                 power_ref, sum_ref):
    t = pl.program_id(0)
    power = frame_power(first_ref[...], second_ref[...], window_ref[...], even_ref, odd_ref)
    power_ref[0] = power
    term = chan_term(rows_ref, power, time2_ref[pl.ds(t, 1), :])

    @pl.when(t == 0)
    def _():
        sum_ref[...] = term

    @pl.when(t > 0)
    def _():
        sum_ref[...] += term


def last_kernel(first_ref, second_ref, window_ref, even_ref, odd_ref, rows_ref, time2_ref,
                sum_ref, old_ref, power_ref, send_ref):
    power = frame_power(first_ref[...], second_ref[...], window_ref[...], even_ref, odd_ref)
    power_ref[0] = power
    total = sum_ref[...] + chan_term(rows_ref, power, time2_ref[FRAMES_HERE - 1:, :])
    total = total[:RANK] + total[RANK:]
    half = CHANS_HERE // 2
    packed = jnp.concatenate([total[:, :half], total[:, half:]], axis=0).T
    per = half // N_TM
    for d in range(N_TM):
        send_ref[d, :per] = packed[d * per:(d + 1) * per]
        send_ref[d, per:] = time2_ref[...]


def chan_kernel(got_ref, gram_freq_ref, start_ref, send_ref, gram_time_ref):
    me = lax.axis_index(TM)
    per = CHANS_HERE // 2 // N_TM
    total = jnp.sum(got_ref[:, :per], axis=0)
    times = got_ref[:, per:].reshape(N_TM * FRAMES_HERE, PACK)
    gram_time = gram_of(times)
    gram_time_ref[...] = gram_time
    penalty, inverse = inverse_of(gram_time * gram_freq_ref[...])
    at = pl.multiple_of(me * per, per)
    top = start_ref[pl.ds(at, per), :]
    bottom = start_ref[pl.ds(at + CHANS_HERE // 2, per), :]
    start = jnp.concatenate([top, bottom], axis=1)
    new = admm(total * SCALE, start, penalty, inverse)
    send_ref[...] = jnp.broadcast_to(new[None], send_ref.shape)


FRAMES_STEP = 4


def freq_kernel(chan_ref, power_ref, time2_ref, part_ref, send_ref, gram_ref, chan_out_ref,
                sides, total):
    step = pl.program_id(0)

    @pl.when(step == 0)
    def _():
        rows = both_halves(chan_ref[...].reshape(CHANS_HERE // 2, PACK))
        chan_out_ref[...] = rows[:, :RANK]
        sides[...] = high_low(rows)
        gram_ref[...] = side_by_side(gram_of(rows)[:RANK])
        total[...] = jnp.zeros_like(total)

    for t in range(FRAMES_STEP):
        part = jnp.dot(power_ref[t], sides[...], preferred_element_type=F32)
        part_ref[t] = part
        total[...] += part * time2_ref[pl.ds(step * FRAMES_STEP + t, 1), :]

    @pl.when(step == FRAMES_HERE // FRAMES_STEP - 1)
    def _():
        whole = total[...]
        packed = side_by_side(whole + pltpu.roll(whole, RANK, 1))
        send_ref[...] = packed.reshape(send_ref.shape)


def rows_kernel(got_ref, gram_ref, send_ref):
    rows = got_ref.shape[1]
    total = jnp.sum(got_ref[...], axis=0)
    for d in range(send_ref.shape[0]):
        send_ref[d, :rows] = total
        send_ref[d, rows:] = gram_ref[...]


def relay_kernel(got_ref, send_ref):
    send_ref[...] = jnp.broadcast_to(jnp.sum(got_ref[...], axis=0)[None], send_ref.shape)


def freq_admm_kernel(got_ref, gram_time_ref, packed_ref, send_ref, gram_chan_ref):
    me = lax.axis_index(TM)
    total = jnp.sum(got_ref[...], axis=0)
    per = BINS // 2 // N_TM
    gram = both_halves(total[per:])
    gram = jnp.concatenate([gram, gram], axis=0)
    gram_chan_ref[...] = gram
    penalty, inverse = inverse_of(gram * gram_time_ref[...])
    start = packed_ref[pl.ds(pl.multiple_of(me * per, per), per), :]
    new = admm(total[:per] * SCALE, start, penalty, inverse)
    send_ref[...] = jnp.broadcast_to(new[None], send_ref.shape)


def time_kernel(freq_ref, part_ref, send_ref, freq_out_ref):
    half = BINS // 2
    rows = both_halves(freq_ref[...].reshape(half, PACK))
    freq_out_ref[pl.ds(0, half, stride=2), :] = rows[:half, :RANK]
    freq_out_ref[pl.ds(1, half, stride=2), :] = rows[half:, :RANK]
    sums = [jnp.sum(part_ref[t] * rows, axis=0, keepdims=True) for t in range(FRAMES_HERE)]
    product = jnp.concatenate(sums, axis=0)
    send_ref[...] = jnp.broadcast_to(product[None], send_ref.shape)


def time_inverse_kernel(freq_ref, gram_chan_ref, inverse_ref, penalty_ref):
    rows = both_halves(freq_ref[...].reshape(BINS // 2, PACK))
    penalty, inverse = inverse_of(gram_of(rows) * gram_chan_ref[...])
    inverse_ref[...] = inverse
    penalty_ref[...] = jnp.full(penalty_ref.shape, penalty, F32)


def time_admm_kernel(got_ref, inverse_ref, penalty_ref, start2_ref, out_ref):
    total = jnp.sum(got_ref[...], axis=0)
    total = total + pltpu.roll(total, RANK, 1)
    new = admm(total * SCALE, start2_ref[...], penalty_ref[...], inverse_ref[...])
    out_ref[...] = new[:, :RANK]


def shape(*dims, dtype=F32):
    return jax.ShapeDtypeStruct(dims, dtype)


def exchanged(parts, axis):
    return lax.all_to_all(parts, axis, split_axis=0, concat_axis=0, tiled=True)


def fixed(*dims):
    return pl.BlockSpec(dims, lambda t: (0,) * len(dims))


def local(samples, start_chan, start_freq, start_time):
    even_table, odd_table = (jnp.asarray(t) for t in half_tables())
    window = jnp.asarray(window_row())
    route = [(i, i - 1) for i in range(1, N_TM)]
    following = lax.ppermute(samples[:, :HALF], TM, route)

    packed_freq, gram_freq, freq_rows, time2 = pl.pallas_call(
        prep_kernel,
        out_shape=(shape(BINS // 2, PACK), shape(PACK, PACK), shape(PACK, BINS, dtype=BF16),
                   shape(FRAMES_HERE, PACK)),
        name="prep",
    )(start_freq, start_time)

    table_specs = [fixed(1, HALF), fixed(BINS, HALF), fixed(BINS, HALF), fixed(PACK, BINS),
                   fixed(FRAMES_HERE, PACK)]
    early = FRAMES_HERE - 1
    power, early_sum = pl.pallas_call(
        early_kernel,
        grid=(early,),
        in_specs=[pl.BlockSpec((CHANS_HERE, HALF), lambda t: (0, t)),
                  pl.BlockSpec((CHANS_HERE, HALF), lambda t: (0, t + 1))] + table_specs,
        out_specs=[pl.BlockSpec((1, BINS, CHANS_HERE), lambda t: (t, 0, 0)),
                   fixed(PACK, CHANS_HERE)],
        out_shape=(shape(FRAMES_HERE, BINS, CHANS_HERE, dtype=BF16), shape(PACK, CHANS_HERE)),
        cost_estimate=pl.CostEstimate(flops=2500000000, bytes_accessed=8000000,
                                      transcendentals=0),
        name="early",
    )(samples, samples, window, even_table, odd_table, freq_rows, time2)

    power, to_chan = pl.pallas_call(
        last_kernel,
        grid=(1,),
        in_specs=[pl.BlockSpec((CHANS_HERE, HALF), lambda t: (0, early)),
                  fixed(CHANS_HERE, HALF)] + table_specs
        + [fixed(PACK, CHANS_HERE), pl.BlockSpec(memory_space=pl.ANY)],
        out_specs=[pl.BlockSpec((1, BINS, CHANS_HERE), lambda t: (early, 0, 0)),
                   fixed(N_TM, 16, PACK)],
        out_shape=(shape(FRAMES_HERE, BINS, CHANS_HERE, dtype=BF16), shape(N_TM, 16, PACK)),
        input_output_aliases={8: 0},
        name="last",
    )(samples, following, window, even_table, odd_table, freq_rows, time2, early_sum, power)

    got = exchanged(to_chan, TM)
    chan_rows, gram_time = pl.pallas_call(
        chan_kernel,
        out_shape=(shape(N_TM, 8, PACK), shape(PACK, PACK)),
        name="chan",
    )(got, gram_freq, start_chan)
    chan_all = exchanged(chan_rows, TM)

    part, to_freq, gram_part, factor_chan = pl.pallas_call(
        freq_kernel,
        grid=(FRAMES_HERE // FRAMES_STEP,),
        in_specs=[fixed(N_TM, 8, PACK),
                  pl.BlockSpec((FRAMES_STEP, BINS, CHANS_HERE), lambda t: (t, 0, 0)),
                  fixed(FRAMES_HERE, PACK)],
        out_specs=[pl.BlockSpec((FRAMES_STEP, BINS, PACK), lambda t: (t, 0, 0)),
                   fixed(N_TM, 16, PACK), fixed(RANK // 2, PACK), fixed(CHANS_HERE, RANK)],
        out_shape=(shape(FRAMES_HERE, BINS, PACK), shape(N_TM, 16, PACK),
                   shape(RANK // 2, PACK), shape(CHANS_HERE, RANK)),
        scratch_shapes=[pltpu.VMEM((CHANS_HERE, PACK), BF16), pltpu.VMEM((BINS, PACK), F32)],
        name="freq",
    )(chan_all, power, time2)

    got = exchanged(to_freq, TM)
    rows = 16 + RANK // 2
    to_z = pl.pallas_call(rows_kernel, out_shape=shape(N_Z, rows, PACK), name="rows")(
        got, gram_part)
    got = exchanged(to_z, "chan_1")
    to_x = pl.pallas_call(relay_kernel, out_shape=shape(N_X, rows, PACK), name="relay")(got)
    got = exchanged(to_x, "chan_0")
    freq_rows_new, gram_chan = pl.pallas_call(
        freq_admm_kernel,
        out_shape=(shape(N_TM, 16, PACK), shape(PACK, PACK)),
        name="freq_admm",
    )(got, gram_time, packed_freq)
    freq_all = exchanged(freq_rows_new, TM)

    to_z, factor_freq = pl.pallas_call(
        time_kernel,
        out_shape=(shape(N_Z, FRAMES_HERE, PACK), shape(BINS, RANK)),
        name="time",
    )(freq_all, part)
    got = exchanged(to_z, "chan_1")
    inverse, penalty = pl.pallas_call(
        time_inverse_kernel,
        out_shape=(shape(PACK, PACK), shape(1, PACK)),
        name="time_inverse",
    )(freq_all, gram_chan)
    to_x = pl.pallas_call(relay_kernel, out_shape=shape(N_X, FRAMES_HERE, PACK),
                          name="relay_time")(got)
    got = exchanged(to_x, "chan_0")
    factor_time = pl.pallas_call(
        time_admm_kernel, out_shape=shape(FRAMES_HERE, RANK), name="time_admm"
    )(got, inverse, penalty, time2)
    return factor_chan, factor_freq, factor_time


def solution(mesh):
    finer = Mesh(mesh.devices.reshape(4, 8, 8, 2), ("chan_0", "chan_1", "tm_0", "tm_1"))
    chan = ("chan_0", "chan_1")
    return jax.shard_map(
        local,
        mesh=finer,
        in_specs=(P(chan, TM), P(chan, None), P(), P(TM, None)),
        out_specs=(P(chan, None), P(), P(TM, None)),
        check_vma=False,
    )
```

```python
import numpy as np
import jax
import jax.numpy as jnp
from jax import lax
from jax.experimental import pallas as pl
from jax.experimental.pallas import tpu as pltpu
from jax.sharding import Mesh
from jax.sharding import PartitionSpec as P

FRAME = 1024
HALF = FRAME // 2
BINS = 512
RANK = 64
ITERS = 5
FRAMES_HERE = 8
CHANS_HERE = 256
PACK = 2 * RANK
TM = ("tm_0", "tm_1")
N_TM = 16
N_X = 4
N_Z = 8
SCALE = 1.0 / (3.0 * FRAME / 8.0)
F32 = jnp.float32
BF16 = jnp.bfloat16
HIGH = lax.Precision.HIGHEST


def half_tables():
    n = np.arange(HALF)[None, :]
    j = np.arange(BINS // 2)[:, None]
    even = 2.0 * np.pi * ((n * (2 * j)) % FRAME) / FRAME
    odd = 2.0 * np.pi * ((n * (2 * j + 1)) % FRAME) / FRAME
    stack = lambda a: np.concatenate([np.cos(a), np.sin(a)], axis=0)
    return stack(even).astype(BF16), stack(odd).astype(BF16)


def window_row():
    n = np.arange(HALF)[None, :]
    return (0.5 - 0.5 * np.cos(2.0 * np.pi * n / FRAME)).astype(np.float32)


def lane_is_low(shape):
    return lax.broadcasted_iota(jnp.int32, shape, 1) < RANK


def both_halves(x):
    other = pltpu.roll(x, RANK, 1)
    low = lane_is_low(x.shape)
    return jnp.concatenate([jnp.where(low, x, other), jnp.where(low, other, x)], axis=0)


def side_by_side(x):
    m = x.shape[0] // 2
    return jnp.where(lane_is_low((m, PACK)), x[:m], x[m:])


def split(x):
    high = x.astype(BF16)
    return high, (x - high.astype(F32)).astype(BF16)


def high_low(x):
    high = x.astype(BF16).astype(F32)
    return jnp.where(lane_is_low(x.shape), high, x - high).astype(BF16)


def doubled(x):
    return jnp.concatenate([x, x], axis=1)


def times(left, right):
    a, b = split(left)
    c, d = split(right)
    both = jnp.concatenate([c, d], axis=1)
    out = jnp.dot(jnp.concatenate([a, b], axis=1), jnp.concatenate([both, both], axis=0),
                  preferred_element_type=F32)
    return out[:, :PACK] + out[:, PACK:]


def times_small(left, right):
    c, d = split(right)
    both = jnp.concatenate([c, d], axis=1)
    out = jnp.dot(high_low(left), jnp.concatenate([both, both], axis=0),
                  preferred_element_type=F32)
    return out[:, :PACK] + out[:, PACK:]


def gram_of(x):
    return times(x.T[:RANK], x)


def inverse_of(gram):
    row = lax.broadcasted_iota(jnp.int32, gram.shape, 0)
    col = lax.broadcasted_iota(jnp.int32, gram.shape, 1)
    eye = jnp.where((row == col) | (row + RANK == col), 1.0, 0.0).astype(F32)
    penalty = jnp.sum(gram * eye) / PACK
    a = gram * (1.0 / penalty) + eye
    mid = RANK / 2.0 + 1.0
    spread = (RANK / 2.0) / mid
    x = eye * (1.0 / mid)
    s = a * (1.0 / mid)
    for step in range(5):
        factor = (2.0 * eye - s) * (1.0 / (1.0 - spread * spread / 2.0))
        spread = (spread * spread / 2.0) / (1.0 - spread * spread / 2.0)
        if step == 0:
            s, x = times_small(s, factor), factor * (1.0 / mid)
        elif step < 4:
            both = times_small(jnp.concatenate([s, x], axis=0), factor)
            s, x = both[:RANK], both[RANK:]
        else:
            x = times_small(x, factor)
    s = times_small(a, x)
    x = times_small(x, 2.0 * eye - s)
    low = lane_is_low(x.shape)
    return penalty, jnp.concatenate([jnp.where(low, x, 0.0), jnp.where(low, 0.0, x)], axis=0)


def admm(product, previous, penalty, inverse):
    scaled = product * (1.0 / penalty)
    carried = previous
    dual = jnp.zeros_like(previous)
    value = previous
    for _ in range(ITERS):
        target = times(scaled + carried, inverse)
        value = target - dual
        dual = jnp.maximum(-value, 0.0)
        carried = jnp.abs(value)
    return jnp.maximum(value, 0.0)


def stacked(x):
    m = x.shape[1] // 2
    return jnp.concatenate([x[:, :m], x[:, m:]], axis=0)


def start_kernel(freq_ref, chan_ref, gram_ref, freq_packed_ref, chan_packed_ref, natural):
    half = BINS // 2
    natural[...] = doubled(freq_ref[...].T)
    even = natural[pl.ds(0, half, stride=2), :]
    odd = natural[pl.ds(1, half, stride=2), :]
    freq_packed_ref[...] = jnp.where(lane_is_low(even.shape), even, odd)
    gram_ref[...] = gram_of(natural[...])
    chan_packed_ref[...] = stacked(chan_ref[...]).T


def frame_power(first, second, window, even_ref, odd_ref):
    first = first.astype(F32) * window
    second = second.astype(F32)
    second = second - second * window
    total = (first + second).astype(BF16)
    change = (first - second).astype(BF16)
    dims = (((1,), (1,)), ((), ()))
    half = BINS // 2
    out = []
    for table, side in ((even_ref, total), (odd_ref, change)):
        wave = lax.dot_general(table[...], side, dims, preferred_element_type=F32)
        out.append((wave[:half] * wave[:half] + wave[half:] * wave[half:]).astype(BF16))
    return jnp.concatenate(out, axis=0)


def chan_term(rows_ref, power, time_row):
    q = jnp.dot(rows_ref[...], power, preferred_element_type=F32)
    row = lax.broadcasted_iota(jnp.int32, (PACK, PACK), 0)
    col = lax.broadcasted_iota(jnp.int32, (PACK, PACK), 1)
    column = jnp.sum(jnp.where(row == col, time_row, 0.0), axis=1, keepdims=True)
    return q * column


EARLY = FRAMES_HERE - 1


def early_kernel(first_ref, second_ref, freq_ref, time_ref, window_ref, even_ref, odd_ref,
                 power_ref, sum_ref, rows_ref, time2_ref, natural):
    t = pl.program_id(0)

    @pl.when(t == 0)
    def _():
        half = BINS // 2
        time2_ref[...] = doubled(time_ref[...])
        natural[...] = doubled(freq_ref[...].T)
        even = natural[pl.ds(0, half, stride=2), :]
        odd = natural[pl.ds(1, half, stride=2), :]
        rows = high_low(jnp.concatenate([even, odd], axis=0))
        rows_ref[...] = rows.astype(F32).T.astype(BF16)
        sum_ref[...] = jnp.zeros_like(sum_ref)

    power = frame_power(first_ref[...], second_ref[...], window_ref[...], even_ref, odd_ref)
    power_ref[0] = power
    sum_ref[...] += chan_term(rows_ref, power, time2_ref[pl.ds(t, 1), :])


def last_kernel(halo_ref, rows_ref, time2_ref, sum_ref, samples_ref, even_in, odd_in, window_ref,
                power_ref, send_ref, held, even_ref, odd_ref, half_sem, even_sem, odd_sem):
    load = pltpu.make_async_copy(samples_ref.at[:, EARLY * HALF:], held, half_sem)
    even_load = pltpu.make_async_copy(even_in, even_ref, even_sem)
    odd_load = pltpu.make_async_copy(odd_in, odd_ref, odd_sem)
    load.start()
    even_load.start()
    odd_load.start()
    load.wait()
    even_load.wait()
    odd_load.wait()
    power = frame_power(held[...], halo_ref[...], window_ref[...], even_ref, odd_ref)
    power_ref[...] = power
    total = sum_ref[...] + chan_term(rows_ref, power, time2_ref[EARLY:, :])
    packed = stacked(total[:RANK] + total[RANK:]).T
    per = CHANS_HERE // 2 // N_TM
    for d in range(N_TM):
        send_ref[d, :per] = packed[d * per:(d + 1) * per]
        send_ref[d, per:] = time2_ref[...]


def chan_kernel(got_ref, gram_freq_ref, start_ref, send_ref, gram_time_ref):
    me = lax.axis_index(TM)
    per = CHANS_HERE // 2 // N_TM
    total = jnp.sum(got_ref[:, :per], axis=0)
    gram_time = gram_of(got_ref[:, per:].reshape(N_TM * FRAMES_HERE, PACK))
    gram_time_ref[...] = gram_time
    penalty, inverse = inverse_of(gram_time * gram_freq_ref[...])
    start = start_ref[pl.ds(pl.multiple_of(me * per, per), per), :]
    new = admm(total * SCALE, start, penalty, inverse)
    send_ref[...] = jnp.broadcast_to(new[None], send_ref.shape)


FIRST_PART = 3


def freq_kernel(chan_ref, time2_ref, last_ref, early_ref, part_ref, send_ref, sides, held, sems):
    loads = [pltpu.make_async_copy(early_ref.at[t], held.at[t], sems.at[t])
             for t in range(EARLY)]
    for load in loads:
        load.start()
    sides[...] = high_low(both_halves(chan_ref[...].reshape(CHANS_HERE // 2, PACK)))
    part_ref[EARLY] = jnp.dot(last_ref[...], sides[...], preferred_element_type=F32)
    for low, high in ((0, FIRST_PART), (FIRST_PART, EARLY)):
        for t in range(low, high):
            loads[t].wait()
        for t in range(low, high):
            part_ref[t] = jnp.dot(held[t], sides[...], preferred_element_type=F32)
    for d in range(N_TM):
        sums = []
        for at in (d * 16, BINS // 2 + d * 16):
            whole = part_ref[0, at:at + 16] * time2_ref[0:1, :]
            for t in range(1, FRAMES_HERE):
                whole = whole + part_ref[t, at:at + 16] * time2_ref[t:t + 1, :]
            sums.append(whole + pltpu.roll(whole, RANK, 1))
        send_ref[d] = jnp.where(lane_is_low((16, PACK)), *sums)


def chan_out_kernel(chan_ref, gram_ref, chan_out_ref):
    packed = chan_ref[...].reshape(CHANS_HERE // 2, PACK)
    gram_ref[...] = side_by_side(gram_of(both_halves(packed)))
    turned = packed.T
    chan_out_ref[...] = jnp.concatenate([turned[:RANK], turned[RANK:]], axis=1)


def spread_kernel(got_ref, gram_ref, send_ref):
    rows = got_ref.shape[1]
    total = jnp.sum(got_ref[...], axis=0)
    for d in range(send_ref.shape[0]):
        send_ref[d, :rows] = total
        send_ref[d, rows:] = gram_ref[...]


def relay_kernel(got_ref, send_ref):
    send_ref[...] = jnp.broadcast_to(jnp.sum(got_ref[...], axis=0)[None], send_ref.shape)


def freq_admm_kernel(got_ref, gram_time_ref, start_ref, send_ref, gram_chan_ref):
    me = lax.axis_index(TM)
    total = jnp.sum(got_ref[...], axis=0)
    per = BINS // 2 // N_TM
    gram = both_halves(total[per:])
    gram_chan_ref[...] = gram
    penalty, inverse = inverse_of(gram * gram_time_ref[...])
    start = start_ref[pl.ds(pl.multiple_of(me * per, per), per), :]
    new = admm(total[:per] * SCALE, start, penalty, inverse)
    send_ref[...] = jnp.broadcast_to(new[None], send_ref.shape)


def time_kernel(freq_ref, part_ref, send_ref):
    rows = both_halves(freq_ref[...].reshape(BINS // 2, PACK))
    sums = [jnp.sum(part_ref[t] * rows, axis=0, keepdims=True) for t in range(FRAMES_HERE)]
    product = jnp.concatenate(sums, axis=0)
    send_ref[...] = jnp.broadcast_to(product[None], send_ref.shape)


def freq_out_kernel(freq_ref, gram_chan_ref, inverse_ref, penalty_ref, freq_out_ref, natural):
    half = BINS // 2
    rows = both_halves(freq_ref[...].reshape(half, PACK))
    natural[pl.ds(0, half, stride=2), :] = rows[:half]
    natural[pl.ds(1, half, stride=2), :] = rows[half:]
    freq_out_ref[...] = natural[...].T[:RANK]
    penalty, inverse = inverse_of(gram_of(rows) * gram_chan_ref[...])
    inverse_ref[...] = inverse
    penalty_ref[...] = jnp.full(penalty_ref.shape, penalty, F32)


def time_admm_kernel(got_ref, inverse_ref, penalty_ref, start2_ref, out_ref):
    total = jnp.sum(got_ref[...], axis=0)
    total = total + pltpu.roll(total, RANK, 1)
    new = admm(total * SCALE, start2_ref[...], penalty_ref[...], inverse_ref[...])
    out_ref[...] = new[:, :RANK]


def shape(*dims, dtype=F32):
    return jax.ShapeDtypeStruct(dims, dtype)


def exchanged(parts, axis):
    return lax.all_to_all(parts, axis, split_axis=0, concat_axis=0, tiled=True)


NEAR = pl.BlockSpec(memory_space=pltpu.VMEM)


def near_call(body, name, outs, args, scratch=(), far=(), outside=(), flops=0, others=(),
              kinds_of_others=()):
    def kind(i, o):
        if i in far:
            return o
        return (pltpu.HBM if i in outside else pltpu.VMEM)(o.shape, o.dtype)

    args = [pltpu.with_memory_space_constraint(a, pltpu.VMEM) for a in args]
    args += [pltpu.with_memory_space_constraint(a, pltpu.HBM) for a in others]
    size = sum(a.size * a.dtype.itemsize for a in list(args) + list(outs))
    away = pl.BlockSpec(memory_space=pltpu.HBM)
    return pl.pallas_call(
        body,
        in_specs=[NEAR] * (len(args) - len(others)) + list(kinds_of_others),
        out_specs=tuple(away if i in outside else NEAR for i in range(len(outs))),
        out_shape=tuple(kind(i, o) for i, o in enumerate(outs)),
        scratch_shapes=list(scratch),
        compiler_params=pltpu.CompilerParams(vmem_limit_bytes=32 * 1024 * 1024),
        cost_estimate=pl.CostEstimate(flops=flops, bytes_accessed=size, transcendentals=0),
        name=name,
    )(*args)


def local(samples, start_chan, start_freq, start_time):
    even_table, odd_table = (jnp.asarray(t) for t in half_tables())
    window = jnp.asarray(window_row())
    route = [(i, i - 1) for i in range(1, N_TM)]
    following = lax.ppermute(samples[:, :HALF], TM, route)
    natural = [pltpu.VMEM((BINS, PACK), F32)]
    table = pltpu.VMEM((BINS, HALF), BF16)
    flag = pltpu.SemaphoreType.DMA
    outside = pl.BlockSpec(memory_space=pltpu.HBM)

    def fixed(*dims):
        return pl.BlockSpec(dims, lambda t: (0,) * len(dims))

    power, early_sum, freq_rows, time2 = pl.pallas_call(
        early_kernel,
        grid=(EARLY,),
        in_specs=[pl.BlockSpec((CHANS_HERE, HALF), lambda t: (0, t)),
                  pl.BlockSpec((CHANS_HERE, HALF), lambda t: (0, t + 1)),
                  fixed(RANK, BINS), fixed(FRAMES_HERE, RANK), fixed(1, HALF),
                  fixed(BINS, HALF), fixed(BINS, HALF)],
        out_specs=[pl.BlockSpec((1, BINS, CHANS_HERE), lambda t: (t, 0, 0)),
                   fixed(PACK, CHANS_HERE), fixed(PACK, BINS), fixed(FRAMES_HERE, PACK)],
        out_shape=(shape(EARLY, BINS, CHANS_HERE, dtype=BF16), shape(PACK, CHANS_HERE),
                   shape(PACK, BINS, dtype=BF16), shape(FRAMES_HERE, PACK)),
        scratch_shapes=natural,
        cost_estimate=pl.CostEstimate(flops=2500000000, bytes_accessed=8000000,
                                      transcendentals=0),
        name="early",
    )(samples, samples, start_freq.T, start_time, window, even_table, odd_table)
    power_last, to_chan = near_call(
        last_kernel, "last", (shape(BINS, CHANS_HERE, dtype=BF16), shape(N_TM, 16, PACK)),
        (following,),
        [pltpu.VMEM((CHANS_HERE, HALF), BF16), table, table, flag(()), flag(()), flag(())],
        far=(1,),
        others=(freq_rows, time2, early_sum, samples, even_table, odd_table, window),
        kinds_of_others=[NEAR] * 3 + [outside] * 3 + [NEAR])

    got = exchanged(to_chan, TM)
    gram_freq, freq_packed, chan_packed = near_call(
        start_kernel, "start",
        (shape(RANK, PACK), shape(BINS // 2, PACK), shape(CHANS_HERE // 2, PACK)),
        (start_freq.T, start_chan.T), natural)
    chan_rows, gram_time = near_call(
        chan_kernel, "chan", (shape(N_TM, 8, PACK), shape(RANK, PACK)),
        (got, gram_freq, chan_packed))
    chan_all = exchanged(chan_rows, TM)

    part, to_freq = near_call(
        freq_kernel, "freq", (shape(FRAMES_HERE, BINS, PACK), shape(N_TM, 16, PACK)),
        (chan_all, time2, power_last),
        [pltpu.VMEM((CHANS_HERE, PACK), BF16), pltpu.VMEM((EARLY, BINS, CHANS_HERE), BF16),
         flag((EARLY,))], far=(1,), others=(power,), kinds_of_others=[outside])
    got = exchanged(to_freq, TM)
    gram_part, chan_out = near_call(
        chan_out_kernel, "chan_out", (shape(RANK // 2, PACK), shape(RANK, CHANS_HERE)),
        (chan_all,), far=(1,))

    rows = 16 + RANK // 2
    (to_z,) = near_call(spread_kernel, "spread", (shape(N_Z, rows, PACK),), (got, gram_part))
    got = exchanged(to_z, "chan_1")
    (to_x,) = near_call(relay_kernel, "relay", (shape(N_X, rows, PACK),), (got,))
    got = exchanged(to_x, "chan_0")
    freq_rows_new, gram_chan = near_call(
        freq_admm_kernel, "freq_admm", (shape(N_TM, 16, PACK), shape(RANK, PACK)),
        (got, gram_time, freq_packed))
    freq_all = exchanged(freq_rows_new, TM)

    (to_z,) = near_call(time_kernel, "time", (shape(N_Z, FRAMES_HERE, PACK),), (freq_all, part),
                        far=(0,))
    got = exchanged(to_z, "chan_1")
    inverse, penalty, freq_out = near_call(
        freq_out_kernel, "freq_out",
        (shape(PACK, PACK), shape(1, PACK), shape(RANK, BINS)), (freq_all, gram_chan),
        natural, far=(2,))
    (to_x,) = near_call(relay_kernel, "relay_time", (shape(N_X, FRAMES_HERE, PACK),), (got,),
                        far=(0,))
    got = exchanged(to_x, "chan_0")
    (factor_time,) = near_call(time_admm_kernel, "time_admm", (shape(FRAMES_HERE, RANK),),
                               (got, inverse, penalty, time2), far=(0,))
    return chan_out.T, freq_out.T, factor_time


def solution(mesh):
    finer = Mesh(mesh.devices.reshape(4, 8, 8, 2), ("chan_0", "chan_1", "tm_0", "tm_1"))
    chan = ("chan_0", "chan_1")
    return jax.shard_map(
        local,
        mesh=finer,
        in_specs=(P(chan, TM), P(chan, None), P(), P(TM, None)),
        out_specs=(P(chan, None), P(), P(TM, None)),
        check_vma=False,
    )
```

```python
import numpy as np
import jax
import jax.numpy as jnp
from jax import lax
from jax.experimental import pallas as pl
from jax.experimental.pallas import tpu as pltpu
from jax.sharding import Mesh
from jax.sharding import PartitionSpec as P

FRAME = 1024
HALF = FRAME // 2
BINS = 512
RANK = 64
ITERS = 5
FRAMES_HERE = 8
CHANS_HERE = 256
PACK = 2 * RANK
TM = ("tm_0", "tm_1")
N_TM = 16
CHAN = ("chan_0", "chan_1")
N_CHAN = 32
SCALE = 1.0 / (3.0 * FRAME / 8.0)
F32 = jnp.float32
BF16 = jnp.bfloat16
HIGH = lax.Precision.HIGHEST


def half_tables():
    n = np.arange(HALF)[None, :]
    j = np.arange(BINS // 2)[:, None]
    even = 2.0 * np.pi * ((n * (2 * j)) % FRAME) / FRAME
    odd = 2.0 * np.pi * ((n * (2 * j + 1)) % FRAME) / FRAME
    stack = lambda a: np.concatenate([np.cos(a), np.sin(a)], axis=0)
    return stack(even).astype(BF16), stack(odd).astype(BF16)


def window_row():
    n = np.arange(HALF)[None, :]
    return (0.5 - 0.5 * np.cos(2.0 * np.pi * n / FRAME)).astype(np.float32)


def lane_is_low(shape):
    return lax.broadcasted_iota(jnp.int32, shape, 1) < RANK


def both_halves(x):
    other = pltpu.roll(x, RANK, 1)
    low = lane_is_low(x.shape)
    return jnp.concatenate([jnp.where(low, x, other), jnp.where(low, other, x)], axis=0)


def side_by_side(x):
    m = x.shape[0] // 2
    return jnp.where(lane_is_low((m, PACK)), x[:m], x[m:])


def split(x):
    high = x.astype(BF16)
    return high, (x - high.astype(F32)).astype(BF16)


def high_low(x):
    high = x.astype(BF16).astype(F32)
    return jnp.where(lane_is_low(x.shape), high, x - high).astype(BF16)


def doubled(x):
    return jnp.concatenate([x, x], axis=1)


def times(left, right):
    a, b = split(left)
    c, d = split(right)
    both = jnp.concatenate([c, d], axis=1)
    out = jnp.dot(jnp.concatenate([a, b], axis=1), jnp.concatenate([both, both], axis=0),
                  preferred_element_type=F32)
    return out[:, :PACK] + out[:, PACK:]


def times_small(left, right):
    c, d = split(right)
    both = jnp.concatenate([c, d], axis=1)
    out = jnp.dot(high_low(left), jnp.concatenate([both, both], axis=0),
                  preferred_element_type=F32)
    return out[:, :PACK] + out[:, PACK:]


def gram_of(x):
    return times(x.T[:RANK], x)


def inverse_of(gram):
    row = lax.broadcasted_iota(jnp.int32, gram.shape, 0)
    col = lax.broadcasted_iota(jnp.int32, gram.shape, 1)
    eye = jnp.where((row == col) | (row + RANK == col), 1.0, 0.0).astype(F32)
    penalty = jnp.sum(gram * eye) / PACK
    a = gram * (1.0 / penalty) + eye
    mid = RANK / 2.0 + 1.0
    spread = (RANK / 2.0) / mid
    x = eye * (1.0 / mid)
    s = a * (1.0 / mid)
    for step in range(5):
        factor = (2.0 * eye - s) * (1.0 / (1.0 - spread * spread / 2.0))
        spread = (spread * spread / 2.0) / (1.0 - spread * spread / 2.0)
        if step == 0:
            s, x = times_small(s, factor), factor * (1.0 / mid)
        elif step < 4:
            both = times_small(jnp.concatenate([s, x], axis=0), factor)
            s, x = both[:RANK], both[RANK:]
        else:
            x = times_small(x, factor)
    s = times_small(a, x)
    x = times_small(x, 2.0 * eye - s)
    low = lane_is_low(x.shape)
    return penalty, jnp.concatenate([jnp.where(low, x, 0.0), jnp.where(low, 0.0, x)], axis=0)


def admm(product, previous, penalty, inverse):
    scaled = product * (1.0 / penalty)
    carried = previous
    dual = jnp.zeros_like(previous)
    value = previous
    for _ in range(ITERS):
        target = times(scaled + carried, inverse)
        value = target - dual
        dual = jnp.maximum(-value, 0.0)
        carried = jnp.abs(value)
    return jnp.maximum(value, 0.0)


def stacked(x):
    m = x.shape[1] // 2
    return jnp.concatenate([x[:, :m], x[:, m:]], axis=0)


def start_kernel(freq_ref, chan_ref, gram_ref, freq_packed_ref, chan_packed_ref, natural):
    half = BINS // 2
    natural[...] = doubled(freq_ref[...].T)
    even = natural[pl.ds(0, half, stride=2), :]
    odd = natural[pl.ds(1, half, stride=2), :]
    freq_packed_ref[...] = jnp.where(lane_is_low(even.shape), even, odd)
    gram_ref[...] = gram_of(natural[...])
    chan_packed_ref[...] = stacked(chan_ref[...]).T


def frame_power(first, second, window, even_ref, odd_ref):
    first = first.astype(F32) * window
    second = second.astype(F32)
    second = second - second * window
    total = (first + second).astype(BF16)
    change = (first - second).astype(BF16)
    dims = (((1,), (1,)), ((), ()))
    half = BINS // 2
    out = []
    for table, side in ((even_ref, total), (odd_ref, change)):
        wave = lax.dot_general(table[...], side, dims, preferred_element_type=F32)
        out.append((wave[:half] * wave[:half] + wave[half:] * wave[half:]).astype(BF16))
    return jnp.concatenate(out, axis=0)


def chan_term(rows_ref, power, time_row):
    q = jnp.dot(rows_ref[...], power, preferred_element_type=F32)
    row = lax.broadcasted_iota(jnp.int32, (PACK, PACK), 0)
    col = lax.broadcasted_iota(jnp.int32, (PACK, PACK), 1)
    column = jnp.sum(jnp.where(row == col, time_row, 0.0), axis=1, keepdims=True)
    return q * column


EARLY = FRAMES_HERE - 1


def early_kernel(first_ref, second_ref, freq_ref, time_ref, window_ref, even_ref, odd_ref,
                 power_ref, sum_ref, rows_ref, time2_ref, natural):
    t = pl.program_id(0)

    @pl.when(t == 0)
    def _():
        half = BINS // 2
        time2_ref[...] = doubled(time_ref[...])
        natural[...] = doubled(freq_ref[...].T)
        even = natural[pl.ds(0, half, stride=2), :]
        odd = natural[pl.ds(1, half, stride=2), :]
        rows = high_low(jnp.concatenate([even, odd], axis=0))
        rows_ref[...] = rows.astype(F32).T.astype(BF16)
        sum_ref[...] = jnp.zeros_like(sum_ref)

    power = frame_power(first_ref[...], second_ref[...], window_ref[...], even_ref, odd_ref)
    power_ref[0] = power
    sum_ref[...] += chan_term(rows_ref, power, time2_ref[pl.ds(t, 1), :])


def last_kernel(halo_ref, rows_ref, time2_ref, sum_ref, samples_ref, even_in, odd_in, window_ref,
                power_ref, send_ref, held, even_ref, odd_ref, half_sem, even_sem, odd_sem):
    load = pltpu.make_async_copy(samples_ref.at[:, EARLY * HALF:], held, half_sem)
    even_load = pltpu.make_async_copy(even_in, even_ref, even_sem)
    odd_load = pltpu.make_async_copy(odd_in, odd_ref, odd_sem)
    load.start()
    even_load.start()
    odd_load.start()
    load.wait()
    even_load.wait()
    odd_load.wait()
    power = frame_power(held[...], halo_ref[...], window_ref[...], even_ref, odd_ref)
    power_ref[...] = power
    total = sum_ref[...] + chan_term(rows_ref, power, time2_ref[EARLY:, :])
    packed = stacked(total[:RANK] + total[RANK:]).T
    per = CHANS_HERE // 2 // N_TM
    for d in range(N_TM):
        send_ref[d, :per] = packed[d * per:(d + 1) * per]
        send_ref[d, per:] = time2_ref[...]


def chan_kernel(got_ref, gram_freq_ref, start_ref, send_ref, gram_time_ref):
    me = lax.axis_index(TM)
    per = CHANS_HERE // 2 // N_TM
    total = jnp.sum(got_ref[:, :per], axis=0)
    gram_time = gram_of(got_ref[:, per:].reshape(N_TM * FRAMES_HERE, PACK))
    gram_time_ref[...] = gram_time
    penalty, inverse = inverse_of(gram_time * gram_freq_ref[...])
    start = start_ref[pl.ds(pl.multiple_of(me * per, per), per), :]
    new = admm(total * SCALE, start, penalty, inverse)
    send_ref[...] = jnp.broadcast_to(new[None], send_ref.shape)


FIRST_PART = 3


def freq_kernel(chan_ref, time2_ref, last_ref, early_ref, part_ref, send_ref, sides, held, sems):
    loads = [pltpu.make_async_copy(early_ref.at[t], held.at[t], sems.at[t])
             for t in range(EARLY)]
    for load in loads:
        load.start()
    sides[...] = high_low(both_halves(chan_ref[...].reshape(CHANS_HERE // 2, PACK)))
    part_ref[EARLY] = jnp.dot(last_ref[...], sides[...], preferred_element_type=F32)
    for low, high in ((0, FIRST_PART), (FIRST_PART, EARLY)):
        for t in range(low, high):
            loads[t].wait()
        for t in range(low, high):
            part_ref[t] = jnp.dot(held[t], sides[...], preferred_element_type=F32)
    for d in range(N_TM):
        sums = []
        for at in (d * 16, BINS // 2 + d * 16):
            whole = part_ref[0, at:at + 16] * time2_ref[0:1, :]
            for t in range(1, FRAMES_HERE):
                whole = whole + part_ref[t, at:at + 16] * time2_ref[t:t + 1, :]
            sums.append(whole + pltpu.roll(whole, RANK, 1))
        send_ref[d] = jnp.where(lane_is_low((16, PACK)), *sums)


def chan_out_kernel(chan_ref, gram_ref, chan_out_ref):
    packed = chan_ref[...].reshape(CHANS_HERE // 2, PACK)
    gram_ref[...] = side_by_side(gram_of(both_halves(packed)))
    turned = packed.T
    chan_out_ref[...] = jnp.concatenate([turned[:RANK], turned[RANK:]], axis=1)


def spread_kernel(got_ref, gram_ref, send_ref):
    me = lax.axis_index(TM)
    rows = got_ref.shape[1]
    total = jnp.sum(got_ref[...], axis=0)
    block = gram_ref[pl.ds(pl.multiple_of(me // (N_TM // 4) * 8, 8), 8), :]
    for d in range(send_ref.shape[0]):
        send_ref[d, :rows] = total
        send_ref[d, rows:] = block


def relay_kernel(got_ref, send_ref):
    send_ref[...] = jnp.broadcast_to(jnp.sum(got_ref[...], axis=0)[None], send_ref.shape)


def freq_admm_kernel(got_ref, gram_time_ref, start_ref, part_ref, send_ref, new_ref,
                     gram_chan_ref):
    rows = BINS // 2 // N_TM
    product = got_ref[:, :rows].reshape(BINS // 2, PACK)
    gram = both_halves(jnp.concatenate(
        [got_ref[d, rows:] for d in range(0, N_TM, N_TM // 4)], axis=0))
    gram_chan_ref[...] = gram
    penalty, inverse = inverse_of(gram * gram_time_ref[...])
    new = admm(product * SCALE, start_ref[...], penalty, inverse)
    new_ref[...] = new
    twice = both_halves(new)
    sums = [jnp.sum(part_ref[t] * twice, axis=0, keepdims=True) for t in range(FRAMES_HERE)]
    product = jnp.concatenate(sums, axis=0)
    send_ref[...] = jnp.broadcast_to(product[None], send_ref.shape)


def freq_out_kernel(freq_ref, gram_chan_ref, inverse_ref, penalty_ref, freq_out_ref, natural):
    half = BINS // 2
    rows = both_halves(freq_ref[...])
    natural[pl.ds(0, half, stride=2), :] = rows[:half]
    natural[pl.ds(1, half, stride=2), :] = rows[half:]
    freq_out_ref[...] = natural[...].T[:RANK]
    penalty, inverse = inverse_of(gram_of(rows) * gram_chan_ref[...])
    inverse_ref[...] = inverse
    penalty_ref[...] = jnp.full(penalty_ref.shape, penalty, F32)


def time_admm_kernel(got_ref, inverse_ref, penalty_ref, start2_ref, out_ref):
    total = jnp.sum(got_ref[...], axis=0)
    total = total + pltpu.roll(total, RANK, 1)
    new = admm(total * SCALE, start2_ref[...], penalty_ref[...], inverse_ref[...])
    out_ref[...] = new[:, :RANK]


def shape(*dims, dtype=F32):
    return jax.ShapeDtypeStruct(dims, dtype)


def exchanged(parts, axis):
    return lax.all_to_all(parts, axis, split_axis=0, concat_axis=0, tiled=True)


NEAR = pl.BlockSpec(memory_space=pltpu.VMEM)


def near_call(body, name, outs, args, scratch=(), far=(), outside=(), flops=0, others=(),
              kinds_of_others=()):
    def kind(i, o):
        if i in far:
            return o
        return (pltpu.HBM if i in outside else pltpu.VMEM)(o.shape, o.dtype)

    args = [pltpu.with_memory_space_constraint(a, pltpu.VMEM) for a in args]
    args += [pltpu.with_memory_space_constraint(a, pltpu.HBM) for a in others]
    size = sum(a.size * a.dtype.itemsize for a in list(args) + list(outs))
    away = pl.BlockSpec(memory_space=pltpu.HBM)
    return pl.pallas_call(
        body,
        in_specs=[NEAR] * (len(args) - len(others)) + list(kinds_of_others),
        out_specs=tuple(away if i in outside else NEAR for i in range(len(outs))),
        out_shape=tuple(kind(i, o) for i, o in enumerate(outs)),
        scratch_shapes=list(scratch),
        compiler_params=pltpu.CompilerParams(vmem_limit_bytes=32 * 1024 * 1024),
        cost_estimate=pl.CostEstimate(flops=flops, bytes_accessed=size, transcendentals=0),
        name=name,
    )(*args)


def local(samples, start_chan, start_freq, start_time):
    even_table, odd_table = (jnp.asarray(t) for t in half_tables())
    window = jnp.asarray(window_row())
    route = [(i, i - 1) for i in range(1, N_TM)]
    following = lax.ppermute(samples[:, :HALF], TM, route)
    natural = [pltpu.VMEM((BINS, PACK), F32)]
    table = pltpu.VMEM((BINS, HALF), BF16)
    flag = pltpu.SemaphoreType.DMA
    outside = pl.BlockSpec(memory_space=pltpu.HBM)

    def fixed(*dims):
        return pl.BlockSpec(dims, lambda t: (0,) * len(dims))

    power, early_sum, freq_rows, time2 = pl.pallas_call(
        early_kernel,
        grid=(EARLY,),
        in_specs=[pl.BlockSpec((CHANS_HERE, HALF), lambda t: (0, t)),
                  pl.BlockSpec((CHANS_HERE, HALF), lambda t: (0, t + 1)),
                  fixed(RANK, BINS), fixed(FRAMES_HERE, RANK), fixed(1, HALF),
                  fixed(BINS, HALF), fixed(BINS, HALF)],
        out_specs=[pl.BlockSpec((1, BINS, CHANS_HERE), lambda t: (t, 0, 0)),
                   fixed(PACK, CHANS_HERE), fixed(PACK, BINS), fixed(FRAMES_HERE, PACK)],
        out_shape=(shape(EARLY, BINS, CHANS_HERE, dtype=BF16), shape(PACK, CHANS_HERE),
                   shape(PACK, BINS, dtype=BF16), shape(FRAMES_HERE, PACK)),
        scratch_shapes=natural,
        cost_estimate=pl.CostEstimate(flops=2500000000, bytes_accessed=8000000,
                                      transcendentals=0),
        name="early",
    )(samples, samples, start_freq.T, start_time, window, even_table, odd_table)
    power_last, to_chan = near_call(
        last_kernel, "last", (shape(BINS, CHANS_HERE, dtype=BF16), shape(N_TM, 16, PACK)),
        (following,),
        [pltpu.VMEM((CHANS_HERE, HALF), BF16), table, table, flag(()), flag(()), flag(())],
        far=(1,),
        others=(freq_rows, time2, early_sum, samples, even_table, odd_table, window),
        kinds_of_others=[NEAR] * 3 + [outside] * 3 + [NEAR])

    got = exchanged(to_chan, TM)
    gram_freq, freq_packed, chan_packed = near_call(
        start_kernel, "start",
        (shape(RANK, PACK), shape(BINS // 2, PACK), shape(CHANS_HERE // 2, PACK)),
        (start_freq.T, start_chan.T), natural)
    chan_rows, gram_time = near_call(
        chan_kernel, "chan", (shape(N_TM, 8, PACK), shape(RANK, PACK)),
        (got, gram_freq, chan_packed))
    chan_all = exchanged(chan_rows, TM)

    part, to_freq = near_call(
        freq_kernel, "freq", (shape(FRAMES_HERE, BINS, PACK), shape(N_TM, 16, PACK)),
        (chan_all, time2, power_last),
        [pltpu.VMEM((CHANS_HERE, PACK), BF16), pltpu.VMEM((EARLY, BINS, CHANS_HERE), BF16),
         flag((EARLY,))], far=(1,), others=(power,), kinds_of_others=[outside])
    got = exchanged(to_freq, TM)
    gram_part, chan_out = near_call(
        chan_out_kernel, "chan_out", (shape(RANK // 2, PACK), shape(RANK, CHANS_HERE)),
        (chan_all,), far=(1,))

    rows = 16 + 8
    (to_all,) = near_call(spread_kernel, "spread", (shape(N_CHAN, rows, PACK),), (got, gram_part))
    got = exchanged(to_all, CHAN)
    (to_tm,) = near_call(relay_kernel, "relay", (shape(N_TM, rows, PACK),), (got,))
    got = exchanged(to_tm, TM)
    to_all, freq_all, gram_chan = near_call(
        freq_admm_kernel, "freq_admm",
        (shape(N_CHAN, FRAMES_HERE, PACK), shape(BINS // 2, PACK), shape(RANK, PACK)),
        (got, gram_time, freq_packed, part), far=(0,))
    got = exchanged(to_all, CHAN)
    inverse, penalty, freq_out = near_call(
        freq_out_kernel, "freq_out",
        (shape(PACK, PACK), shape(1, PACK), shape(RANK, BINS)), (freq_all, gram_chan),
        natural, far=(2,))
    (factor_time,) = near_call(time_admm_kernel, "time_admm", (shape(FRAMES_HERE, RANK),),
                               (got, inverse, penalty, time2), far=(0,))
    return chan_out.T, freq_out.T, factor_time


def solution(mesh):
    finer = Mesh(mesh.devices.reshape(4, 8, 8, 2), ("chan_0", "chan_1", "tm_0", "tm_1"))
    return jax.shard_map(
        local,
        mesh=finer,
        in_specs=(P(CHAN, TM), P(CHAN, None), P(), P(TM, None)),
        out_specs=(P(CHAN, None), P(), P(TM, None)),
        check_vma=False,
    )
```

```python
import numpy as np
import jax
import jax.numpy as jnp
from jax import lax
from jax.experimental import pallas as pl
from jax.experimental.pallas import tpu as pltpu
from jax.sharding import Mesh
from jax.sharding import PartitionSpec as P

FRAME = 1024
HALF = FRAME // 2
BINS = 512
RANK = 64
ITERS = 5
FRAMES_HERE = 8
CHANS_HERE = 256
PACK = 2 * RANK
TM = ("tm_0", "tm_1")
N_TM = 16
CHAN = ("chan_0", "chan_1")
N_CHAN = 32
SCALE = 1.0 / (3.0 * FRAME / 8.0)
F32 = jnp.float32
BF16 = jnp.bfloat16
HIGH = lax.Precision.HIGHEST


def half_tables():
    n = np.arange(HALF)[None, :]
    j = np.arange(BINS // 2)[:, None]
    even = 2.0 * np.pi * ((n * (2 * j)) % FRAME) / FRAME
    odd = 2.0 * np.pi * ((n * (2 * j + 1)) % FRAME) / FRAME
    stack = lambda a: np.concatenate([np.cos(a), np.sin(a)], axis=0)
    return stack(even).astype(BF16), stack(odd).astype(BF16)


def window_row():
    n = np.arange(HALF)[None, :]
    return (0.5 - 0.5 * np.cos(2.0 * np.pi * n / FRAME)).astype(np.float32)


def lane_is_low(shape):
    return lax.broadcasted_iota(jnp.int32, shape, 1) < RANK


def both_halves(x):
    other = pltpu.roll(x, RANK, 1)
    low = lane_is_low(x.shape)
    return jnp.concatenate([jnp.where(low, x, other), jnp.where(low, other, x)], axis=0)


def side_by_side(x):
    m = x.shape[0] // 2
    return jnp.where(lane_is_low((m, PACK)), x[:m], x[m:])


def split(x):
    high = x.astype(BF16)
    return high, (x - high.astype(F32)).astype(BF16)


def high_low(x):
    high = x.astype(BF16).astype(F32)
    return jnp.where(lane_is_low(x.shape), high, x - high).astype(BF16)


def doubled(x):
    return jnp.concatenate([x, x], axis=1)


def times(left, right):
    a, b = split(left)
    c, d = split(right)
    both = jnp.concatenate([c, d], axis=1)
    out = jnp.dot(jnp.concatenate([a, b], axis=1), jnp.concatenate([both, both], axis=0),
                  preferred_element_type=F32)
    return out[:, :PACK] + out[:, PACK:]


def times_small(left, right):
    c, d = split(right)
    both = jnp.concatenate([c, d], axis=1)
    out = jnp.dot(high_low(left), jnp.concatenate([both, both], axis=0),
                  preferred_element_type=F32)
    return out[:, :PACK] + out[:, PACK:]


def gram_of(x):
    return times(x.T[:RANK], x)


def inverse_of(gram):
    row = lax.broadcasted_iota(jnp.int32, gram.shape, 0)
    col = lax.broadcasted_iota(jnp.int32, gram.shape, 1)
    eye = jnp.where((row == col) | (row + RANK == col), 1.0, 0.0).astype(F32)
    penalty = jnp.sum(gram * eye) / PACK
    a = gram * (1.0 / penalty) + eye
    mid = RANK / 2.0 + 1.0
    spread = (RANK / 2.0) / mid
    x = eye * (1.0 / mid)
    s = a * (1.0 / mid)
    for step in range(5):
        factor = (2.0 * eye - s) * (1.0 / (1.0 - spread * spread / 2.0))
        spread = (spread * spread / 2.0) / (1.0 - spread * spread / 2.0)
        if step == 0:
            s, x = times_small(s, factor), factor * (1.0 / mid)
        elif step < 4:
            both = times_small(jnp.concatenate([s, x], axis=0), factor)
            s, x = both[:RANK], both[RANK:]
        else:
            x = times_small(x, factor)
    s = times_small(a, x)
    x = times_small(x, 2.0 * eye - s)
    low = lane_is_low(x.shape)
    return penalty, jnp.concatenate([jnp.where(low, x, 0.0), jnp.where(low, 0.0, x)], axis=0)


def admm(product, previous, penalty, inverse):
    scaled = product * (1.0 / penalty)
    carried = previous
    dual = jnp.zeros_like(previous)
    value = previous
    for _ in range(ITERS):
        target = times(scaled + carried, inverse)
        value = target - dual
        dual = jnp.maximum(-value, 0.0)
        carried = jnp.abs(value)
    return jnp.maximum(value, 0.0)


def stacked(x):
    m = x.shape[1] // 2
    return jnp.concatenate([x[:, :m], x[:, m:]], axis=0)


def start_kernel(freq_ref, chan_ref, gram_ref, freq_packed_ref, chan_packed_ref, natural):
    half = BINS // 2
    natural[...] = doubled(freq_ref[...].T)
    even = natural[pl.ds(0, half, stride=2), :]
    odd = natural[pl.ds(1, half, stride=2), :]
    freq_packed_ref[...] = jnp.where(lane_is_low(even.shape), even, odd)
    gram_ref[...] = gram_of(natural[...])
    chan_packed_ref[...] = stacked(chan_ref[...]).T


def frame_power(first, second, window, even_ref, odd_ref):
    first = first.astype(F32) * window
    second = second.astype(F32)
    second = second - second * window
    total = (first + second).astype(BF16)
    change = (first - second).astype(BF16)
    dims = (((1,), (1,)), ((), ()))
    half = BINS // 2
    out = []
    for table, side in ((even_ref, total), (odd_ref, change)):
        wave = lax.dot_general(table[...], side, dims, preferred_element_type=F32)
        out.append((wave[:half] * wave[:half] + wave[half:] * wave[half:]).astype(BF16))
    return jnp.concatenate(out, axis=0)


def chan_term(rows_ref, power, time_row):
    q = jnp.dot(rows_ref[...], power, preferred_element_type=F32)
    row = lax.broadcasted_iota(jnp.int32, (PACK, PACK), 0)
    col = lax.broadcasted_iota(jnp.int32, (PACK, PACK), 1)
    column = jnp.sum(jnp.where(row == col, time_row, 0.0), axis=1, keepdims=True)
    return q * column


EARLY = FRAMES_HERE - 1


def early_kernel(first_ref, second_ref, freq_ref, time_ref, window_ref, even_ref, odd_ref,
                 power_ref, sum_ref, rows_ref, time2_ref, natural):
    t = pl.program_id(0)

    @pl.when(t == 0)
    def _():
        half = BINS // 2
        time2_ref[...] = doubled(time_ref[...])
        natural[...] = doubled(freq_ref[...].T)
        even = natural[pl.ds(0, half, stride=2), :]
        odd = natural[pl.ds(1, half, stride=2), :]
        rows = high_low(jnp.concatenate([even, odd], axis=0))
        rows_ref[...] = rows.astype(F32).T.astype(BF16)
        sum_ref[...] = jnp.zeros_like(sum_ref)

    power = frame_power(first_ref[...], second_ref[...], window_ref[...], even_ref, odd_ref)
    power_ref[0] = power
    sum_ref[...] += chan_term(rows_ref, power, time2_ref[pl.ds(t, 1), :])


def last_kernel(halo_ref, even_ref, odd_ref, samples_ref, window_in, rows_in, time2_in, sum_in,
                power_ref, send_ref, held, window_ref, rows_ref, time2_ref, sum_ref, sems):
    pairs = ((samples_ref.at[:, EARLY * HALF:], held), (window_in, window_ref),
             (rows_in, rows_ref), (time2_in, time2_ref), (sum_in, sum_ref))
    loads = [pltpu.make_async_copy(*pair, sems.at[i]) for i, pair in enumerate(pairs)]
    for load in loads:
        load.start()
    for load in loads:
        load.wait()
    power = frame_power(held[...], halo_ref[...], window_ref[...], even_ref, odd_ref)
    power_ref[...] = power
    total = sum_ref[...] + chan_term(rows_ref, power, time2_ref[EARLY:, :])
    packed = stacked(total[:RANK] + total[RANK:]).T
    per = CHANS_HERE // 2 // N_TM
    for d in range(N_TM):
        send_ref[d, :per] = packed[d * per:(d + 1) * per]
        send_ref[d, per:] = time2_ref[...]


def head_kernel(samples_ref, out_ref, sem):
    load = pltpu.make_async_copy(samples_ref.at[:, :HALF], out_ref, sem)
    load.start()
    load.wait()


def chan_kernel(got_ref, gram_freq_ref, start_ref, send_ref, gram_time_ref):
    me = lax.axis_index(TM)
    per = CHANS_HERE // 2 // N_TM
    total = jnp.sum(got_ref[:, :per], axis=0)
    gram_time = gram_of(got_ref[:, per:].reshape(N_TM * FRAMES_HERE, PACK))
    gram_time_ref[...] = gram_time
    penalty, inverse = inverse_of(gram_time * gram_freq_ref[...])
    start = start_ref[pl.ds(pl.multiple_of(me * per, per), per), :]
    new = admm(total * SCALE, start, penalty, inverse)
    send_ref[...] = jnp.broadcast_to(new[None], send_ref.shape)


FIRST_PART = 3
TILE = 256


def freq_kernel(chan_ref, time2_ref, last_ref, early_ref, part_ref, send_ref, sides, held, sems):
    loads = [pltpu.make_async_copy(early_ref.at[t], held.at[t], sems.at[t])
             for t in range(EARLY)]
    for load in loads:
        load.start()
    side = high_low(both_halves(chan_ref[...].reshape(CHANS_HERE // 2, PACK)))
    sides[...] = jnp.concatenate([side, side], axis=1)
    order = [EARLY] + list(range(EARLY))

    def body(*accs):
        for m in (0, 1):
            pltpu.matmul_push_rhs(sides[...], 0, m)

        def multiply(i):
            t, m = order[i], i % 2
            power = last_ref[...] if t == EARLY else held[t]
            pltpu.matmul_acc_lhs(accs[i % 4], power, load_staged_rhs=0 if i < 2 else None)

        def collect(i):
            part_ref[order[i]] = pltpu.matmul_pop(accs[i % 4])[:, :PACK]

        for i in range(FRAMES_HERE):
            if i == 1:
                for load in loads[:FIRST_PART]:
                    load.wait()
            if i == 1 + FIRST_PART:
                for load in loads[FIRST_PART:]:
                    load.wait()
            multiply(i)
            if i >= 2:
                collect(i - 2)
        collect(FRAMES_HERE - 2)
        collect(FRAMES_HERE - 1)

    pl.run_scoped(body, *[pltpu.ACC(m)((BINS, TILE), F32) for m in (0, 1, 0, 1)])
    for d in range(N_TM):
        sums = []
        for at in (d * 16, BINS // 2 + d * 16):
            whole = part_ref[0, at:at + 16] * time2_ref[0:1, :]
            for t in range(1, FRAMES_HERE):
                whole = whole + part_ref[t, at:at + 16] * time2_ref[t:t + 1, :]
            sums.append(whole + pltpu.roll(whole, RANK, 1))
        send_ref[d] = jnp.where(lane_is_low((16, PACK)), *sums)


def chan_out_kernel(chan_ref, gram_ref, chan_out_ref):
    packed = chan_ref[...].reshape(CHANS_HERE // 2, PACK)
    gram_ref[...] = side_by_side(gram_of(both_halves(packed)))
    turned = packed.T
    chan_out_ref[...] = jnp.concatenate([turned[:RANK], turned[RANK:]], axis=1)


def spread_kernel(got_ref, gram_ref, send_ref):
    me = lax.axis_index(TM)
    rows = got_ref.shape[1]
    total = jnp.sum(got_ref[...], axis=0)
    block = gram_ref[pl.ds(pl.multiple_of(me // (N_TM // 4) * 8, 8), 8), :]
    for d in range(send_ref.shape[0]):
        send_ref[d, :rows] = total
        send_ref[d, rows:] = block


def relay_kernel(got_ref, send_ref):
    send_ref[...] = jnp.broadcast_to(jnp.sum(got_ref[...], axis=0)[None], send_ref.shape)


def freq_admm_kernel(got_ref, gram_time_ref, start_ref, part_ref, send_ref, new_ref,
                     gram_chan_ref):
    rows = BINS // 2 // N_TM
    product = got_ref[:, :rows].reshape(BINS // 2, PACK)
    gram = both_halves(jnp.concatenate(
        [got_ref[d, rows:] for d in range(0, N_TM, N_TM // 4)], axis=0))
    gram_chan_ref[...] = gram
    penalty, inverse = inverse_of(gram * gram_time_ref[...])
    new = admm(product * SCALE, start_ref[...], penalty, inverse)
    new_ref[...] = new
    twice = both_halves(new)
    sums = [jnp.sum(part_ref[t] * twice, axis=0, keepdims=True) for t in range(FRAMES_HERE)]
    product = jnp.concatenate(sums, axis=0)
    send_ref[...] = jnp.broadcast_to(product[None], send_ref.shape)


def freq_out_kernel(freq_ref, gram_chan_ref, inverse_ref, penalty_ref, freq_out_ref, natural):
    half = BINS // 2
    rows = both_halves(freq_ref[...])
    natural[pl.ds(0, half, stride=2), :] = rows[:half]
    natural[pl.ds(1, half, stride=2), :] = rows[half:]
    freq_out_ref[...] = natural[...].T[:RANK]
    penalty, inverse = inverse_of(gram_of(rows) * gram_chan_ref[...])
    inverse_ref[...] = inverse
    penalty_ref[...] = jnp.full(penalty_ref.shape, penalty, F32)


def time_admm_kernel(got_ref, inverse_ref, penalty_ref, start2_ref, out_ref):
    total = jnp.sum(got_ref[...], axis=0)
    total = total + pltpu.roll(total, RANK, 1)
    new = admm(total * SCALE, start2_ref[...], penalty_ref[...], inverse_ref[...])
    out_ref[...] = new[:, :RANK]


def shape(*dims, dtype=F32):
    return jax.ShapeDtypeStruct(dims, dtype)


def exchanged(parts, axis):
    return lax.all_to_all(parts, axis, split_axis=0, concat_axis=0, tiled=True)


NEAR = pl.BlockSpec(memory_space=pltpu.VMEM)


def near_call(body, name, outs, args, scratch=(), far=(), outside=(), flops=0, others=(),
              kinds_of_others=()):
    def kind(i, o):
        if i in far:
            return o
        return (pltpu.HBM if i in outside else pltpu.VMEM)(o.shape, o.dtype)

    args = [pltpu.with_memory_space_constraint(a, pltpu.VMEM) for a in args]
    args += [pltpu.with_memory_space_constraint(a, pltpu.HBM) for a in others]
    size = sum(a.size * a.dtype.itemsize for a in list(args) + list(outs))
    away = pl.BlockSpec(memory_space=pltpu.HBM)
    return pl.pallas_call(
        body,
        in_specs=[NEAR] * (len(args) - len(others)) + list(kinds_of_others),
        out_specs=tuple(away if i in outside else NEAR for i in range(len(outs))),
        out_shape=tuple(kind(i, o) for i, o in enumerate(outs)),
        scratch_shapes=list(scratch),
        compiler_params=pltpu.CompilerParams(vmem_limit_bytes=32 * 1024 * 1024),
        cost_estimate=pl.CostEstimate(flops=flops, bytes_accessed=size, transcendentals=0),
        name=name,
    )(*args)


def local(samples, start_chan, start_freq, start_time):
    even_table, odd_table = (
        pltpu.with_memory_space_constraint(jnp.asarray(t), pltpu.VMEM) for t in half_tables())
    window = jnp.asarray(window_row())
    flag = pltpu.SemaphoreType.DMA
    outside = pl.BlockSpec(memory_space=pltpu.HBM)
    (head,) = near_call(head_kernel, "head", (shape(CHANS_HERE, HALF, dtype=BF16),), (),
                        [flag(())], others=(samples,), kinds_of_others=[outside])
    route = [(i, i - 1) for i in range(1, N_TM)]
    following = lax.ppermute(head, TM, route)
    natural = [pltpu.VMEM((BINS, PACK), F32)]

    def fixed(*dims):
        return pl.BlockSpec(dims, lambda t: (0,) * len(dims))

    power, early_sum, freq_rows, time2 = pl.pallas_call(
        early_kernel,
        grid=(EARLY,),
        in_specs=[pl.BlockSpec((CHANS_HERE, HALF), lambda t: (0, t)),
                  pl.BlockSpec((CHANS_HERE, HALF), lambda t: (0, t + 1)),
                  fixed(RANK, BINS), fixed(FRAMES_HERE, RANK), fixed(1, HALF),
                  NEAR, NEAR],
        out_specs=[pl.BlockSpec((1, BINS, CHANS_HERE), lambda t: (t, 0, 0)),
                   fixed(PACK, CHANS_HERE), fixed(PACK, BINS), fixed(FRAMES_HERE, PACK)],
        out_shape=(shape(EARLY, BINS, CHANS_HERE, dtype=BF16), shape(PACK, CHANS_HERE),
                   shape(PACK, BINS, dtype=BF16), shape(FRAMES_HERE, PACK)),
        scratch_shapes=natural,
        cost_estimate=pl.CostEstimate(flops=2500000000, bytes_accessed=8000000,
                                      transcendentals=0),
        name="early",
    )(samples, samples, start_freq.T, start_time, window, even_table, odd_table)
    power_last, to_chan = near_call(
        last_kernel, "last", (shape(BINS, CHANS_HERE, dtype=BF16), shape(N_TM, 16, PACK)),
        (following, even_table, odd_table),
        [pltpu.VMEM((CHANS_HERE, HALF), BF16), pltpu.VMEM((1, HALF), F32),
         pltpu.VMEM((PACK, BINS), BF16), pltpu.VMEM((FRAMES_HERE, PACK), F32),
         pltpu.VMEM((PACK, CHANS_HERE), F32), flag((5,))],
        far=(1,), others=(samples, window, freq_rows, time2, early_sum),
        kinds_of_others=[outside] * 5)

    got = exchanged(to_chan, TM)
    gram_freq, freq_packed, chan_packed = near_call(
        start_kernel, "start",
        (shape(RANK, PACK), shape(BINS // 2, PACK), shape(CHANS_HERE // 2, PACK)),
        (start_freq.T, start_chan.T), natural)
    chan_rows, gram_time = near_call(
        chan_kernel, "chan", (shape(N_TM, 8, PACK), shape(RANK, PACK)),
        (got, gram_freq, chan_packed))
    chan_all = exchanged(chan_rows, TM)

    part, to_freq = near_call(
        freq_kernel, "freq", (shape(FRAMES_HERE, BINS, PACK), shape(N_TM, 16, PACK)),
        (chan_all, time2, power_last),
        [pltpu.VMEM((CHANS_HERE, TILE), BF16), pltpu.VMEM((EARLY, BINS, CHANS_HERE), BF16),
         flag((EARLY,))], far=(1,), others=(power,), kinds_of_others=[outside])
    got = exchanged(to_freq, TM)
    gram_part, chan_out = near_call(
        chan_out_kernel, "chan_out", (shape(RANK // 2, PACK), shape(RANK, CHANS_HERE)),
        (chan_all,), far=(1,))

    rows = 16 + 8
    (to_all,) = near_call(spread_kernel, "spread", (shape(N_CHAN, rows, PACK),), (got, gram_part))
    got = exchanged(to_all, CHAN)
    (to_tm,) = near_call(relay_kernel, "relay", (shape(N_TM, rows, PACK),), (got,))
    got = exchanged(to_tm, TM)
    to_all, freq_all, gram_chan = near_call(
        freq_admm_kernel, "freq_admm",
        (shape(N_CHAN, FRAMES_HERE, PACK), shape(BINS // 2, PACK), shape(RANK, PACK)),
        (got, gram_time, freq_packed, part), far=(0,))
    got = exchanged(to_all, CHAN)
    inverse, penalty, freq_out = near_call(
        freq_out_kernel, "freq_out",
        (shape(PACK, PACK), shape(1, PACK), shape(RANK, BINS)), (freq_all, gram_chan),
        natural, far=(2,))
    (factor_time,) = near_call(time_admm_kernel, "time_admm", (shape(FRAMES_HERE, RANK),),
                               (got, inverse, penalty, time2), far=(0,))
    return chan_out.T, freq_out.T, factor_time


def solution(mesh):
    finer = Mesh(mesh.devices.reshape(4, 8, 8, 2), ("chan_0", "chan_1", "tm_0", "tm_1"))
    return jax.shard_map(
        local,
        mesh=finer,
        in_specs=(P(CHAN, TM), P(CHAN, None), P(), P(TM, None)),
        out_specs=(P(CHAN, None), P(), P(TM, None)),
        check_vma=False,
    )
```

```python
import numpy as np
import jax
import jax.numpy as jnp
from jax import lax
from jax.experimental import pallas as pl
from jax.experimental.pallas import tpu as pltpu
from jax.sharding import Mesh
from jax.sharding import PartitionSpec as P

FRAME = 1024
HALF = FRAME // 2
BINS = 512
RANK = 64
ITERS = 5
FRAMES_HERE = 8
QUAD = 4
CHANS_HERE = 256
PACK = 2 * RANK
TM = ("tm_0", "tm_1")
N_TM = 16
CHAN = ("chan_0", "chan_1")
N_CHAN = 32
SCALE = 1.0 / (3.0 * FRAME / 8.0)
F32 = jnp.float32
BF16 = jnp.bfloat16
HIGH = lax.Precision.HIGHEST


def half_tables():
    n = np.arange(HALF)[None, :]
    j = np.arange(BINS // 2)[:, None]
    even = 2.0 * np.pi * ((n * (2 * j)) % FRAME) / FRAME
    odd = 2.0 * np.pi * ((n * (2 * j + 1)) % FRAME) / FRAME
    stack = lambda a: np.concatenate([np.cos(a), np.sin(a)], axis=0)
    return stack(even).astype(BF16), stack(odd).astype(BF16)


def window_row():
    n = np.arange(HALF)[None, :]
    return (0.5 - 0.5 * np.cos(2.0 * np.pi * n / FRAME)).astype(np.float32)


def lane_is_low(shape):
    return lax.broadcasted_iota(jnp.int32, shape, 1) < RANK


def both_halves(x):
    other = pltpu.roll(x, RANK, 1)
    low = lane_is_low(x.shape)
    return jnp.concatenate([jnp.where(low, x, other), jnp.where(low, other, x)], axis=0)


def side_by_side(x):
    m = x.shape[0] // 2
    return jnp.where(lane_is_low((m, PACK)), x[:m], x[m:])


def split(x):
    high = x.astype(BF16)
    return high, (x - high.astype(F32)).astype(BF16)


def high_low(x):
    high = x.astype(BF16).astype(F32)
    return jnp.where(lane_is_low(x.shape), high, x - high).astype(BF16)


def doubled(x):
    return jnp.concatenate([x, x], axis=1)


def times(left, right):
    a, b = split(left)
    c, d = split(right)
    both = jnp.concatenate([c, d], axis=1)
    out = jnp.dot(jnp.concatenate([a, b], axis=1), jnp.concatenate([both, both], axis=0),
                  preferred_element_type=F32)
    return out[:, :PACK] + out[:, PACK:]


def times_small(left, right):
    c, d = split(right)
    both = jnp.concatenate([c, d], axis=1)
    out = jnp.dot(high_low(left), jnp.concatenate([both, both], axis=0),
                  preferred_element_type=F32)
    return out[:, :PACK] + out[:, PACK:]


def gram_of(x):
    return times(x.T[:RANK], x)


def inverse_of(gram):
    row = lax.broadcasted_iota(jnp.int32, gram.shape, 0)
    col = lax.broadcasted_iota(jnp.int32, gram.shape, 1)
    eye = jnp.where((row == col) | (row + RANK == col), 1.0, 0.0).astype(F32)
    penalty = jnp.sum(gram * eye) / PACK
    a = gram * (1.0 / penalty) + eye
    mid = RANK / 2.0 + 1.0
    spread = (RANK / 2.0) / mid
    x = eye * (1.0 / mid)
    s = a * (1.0 / mid)
    for step in range(5):
        factor = (2.0 * eye - s) * (1.0 / (1.0 - spread * spread / 2.0))
        spread = (spread * spread / 2.0) / (1.0 - spread * spread / 2.0)
        if step == 0:
            s, x = times_small(s, factor), factor * (1.0 / mid)
        elif step < 4:
            both = times_small(jnp.concatenate([s, x], axis=0), factor)
            s, x = both[:RANK], both[RANK:]
        else:
            x = times_small(x, factor)
    s = times_small(a, x)
    x = times_small(x, 2.0 * eye - s)
    low = lane_is_low(x.shape)
    return penalty, jnp.concatenate([jnp.where(low, x, 0.0), jnp.where(low, 0.0, x)], axis=0)


def admm(product, previous, penalty, inverse):
    scaled = product * (1.0 / penalty)
    carried = previous
    dual = jnp.zeros_like(previous)
    value = previous
    for _ in range(ITERS):
        target = times(scaled + carried, inverse)
        value = target - dual
        dual = jnp.maximum(-value, 0.0)
        carried = jnp.abs(value)
    return jnp.maximum(value, 0.0)


def stacked(x):
    m = x.shape[1] // 2
    return jnp.concatenate([x[:, :m], x[:, m:]], axis=0)


def start_kernel(freq_ref, chan_ref, gram_ref, freq_packed_ref, chan_packed_ref, natural):
    half = BINS // 2
    natural[...] = doubled(freq_ref[...].T)
    even = natural[pl.ds(0, half, stride=2), :]
    odd = natural[pl.ds(1, half, stride=2), :]
    freq_packed_ref[...] = jnp.where(lane_is_low(even.shape), even, odd)
    gram_ref[...] = gram_of(natural[...])
    chan_packed_ref[...] = stacked(chan_ref[...]).T


def frame_power(first, second, window, even_ref, odd_ref):
    first = first.astype(F32) * window
    second = second.astype(F32)
    second = second - second * window
    total = (first + second).astype(BF16)
    change = (first - second).astype(BF16)
    dims = (((1,), (1,)), ((), ()))
    half = BINS // 2
    out = []
    for table, side in ((even_ref, total), (odd_ref, change)):
        wave = lax.dot_general(table[...], side, dims, preferred_element_type=F32)
        out.append((wave[:half] * wave[:half] + wave[half:] * wave[half:]).astype(BF16))
    return jnp.concatenate(out, axis=0)


def chan_term(rows_ref, power, time_row):
    q = jnp.dot(rows_ref[...], power, preferred_element_type=F32)
    row = lax.broadcasted_iota(jnp.int32, (PACK, PACK), 0)
    col = lax.broadcasted_iota(jnp.int32, (PACK, PACK), 1)
    column = jnp.sum(jnp.where(row == col, time_row, 0.0), axis=1, keepdims=True)
    return q * column


EARLY = FRAMES_HERE - 1


def early_kernel(first_ref, second_ref, freq_ref, time_ref, window_ref, even_ref, odd_ref,
                 power_ref, sum_ref, rows_ref, time2_ref, natural):
    t = pl.program_id(0)

    @pl.when(t == 0)
    def _():
        half = BINS // 2
        time2_ref[...] = doubled(time_ref[...])
        natural[...] = doubled(freq_ref[...].T)
        even = natural[pl.ds(0, half, stride=2), :]
        odd = natural[pl.ds(1, half, stride=2), :]
        rows = high_low(jnp.concatenate([even, odd], axis=0))
        rows_ref[...] = rows.astype(F32).T.astype(BF16)
        sum_ref[...] = jnp.zeros_like(sum_ref)

    power = frame_power(first_ref[...], second_ref[...], window_ref[...], even_ref, odd_ref)
    power_ref[0] = power
    sum_ref[...] += chan_term(rows_ref, power, time2_ref[pl.ds(t, 1), :])


def last_kernel(halo_ref, even_ref, odd_ref, samples_ref, window_in, rows_in, time2_in, sum_in,
                power_ref, send_ref, held, window_ref, rows_ref, time2_ref, sum_ref, sems):
    pairs = ((samples_ref.at[:, EARLY * HALF:], held), (window_in, window_ref),
             (rows_in, rows_ref), (time2_in, time2_ref), (sum_in, sum_ref))
    loads = [pltpu.make_async_copy(*pair, sems.at[i]) for i, pair in enumerate(pairs)]
    for load in loads:
        load.start()
    for load in loads:
        load.wait()
    power = frame_power(held[...], halo_ref[...], window_ref[...], even_ref, odd_ref)
    power_ref[...] = power
    total = sum_ref[...] + chan_term(rows_ref, power, time2_ref[EARLY:, :])
    packed = stacked(total[:RANK] + total[RANK:]).T
    per = CHANS_HERE // 2 // N_TM
    times = side_by_side(time2_ref[...])
    for d in range(N_TM):
        for i in range(per // QUAD):
            send_ref[d, i] = packed[d * per + i * QUAD:d * per + (i + 1) * QUAD]
        send_ref[d, per // QUAD] = times


def head_kernel(samples_ref, out_ref, sem):
    load = pltpu.make_async_copy(samples_ref.at[:, :HALF], out_ref, sem)
    load.start()
    load.wait()


def chan_kernel(got_ref, gram_freq_ref, start_ref, send_ref, gram_time_ref):
    me = lax.axis_index(TM)
    per = CHANS_HERE // 2 // N_TM
    blocks = per // QUAD
    total = jnp.concatenate(
        [sum(got_ref[d, i] for d in range(N_TM)) for i in range(blocks)], axis=0)
    times = jnp.concatenate([got_ref[d, blocks] for d in range(N_TM)], axis=0)
    gram_time = gram_of(both_halves(times))
    gram_time_ref[...] = gram_time
    penalty, inverse = inverse_of(gram_time * gram_freq_ref[...])
    start = start_ref[pl.ds(pl.multiple_of(me * per, per), per), :]
    new = admm(total * SCALE, start, penalty, inverse)
    send_ref[...] = jnp.broadcast_to(new[None], send_ref.shape)


FIRST_PART = 3
TILE = 256


def freq_kernel(chan_ref, time2_ref, last_ref, early_ref, part_ref, send_ref, sides, held, sems):
    loads = [pltpu.make_async_copy(early_ref.at[t], held.at[t], sems.at[t])
             for t in range(EARLY)]
    for load in loads:
        load.start()
    side = high_low(both_halves(chan_ref[...].reshape(CHANS_HERE // 2, PACK)))
    sides[...] = jnp.concatenate([side, side], axis=1)
    order = [EARLY] + list(range(EARLY))

    def body(*accs):
        for m in (0, 1):
            pltpu.matmul_push_rhs(sides[...], 0, m)

        def multiply(i):
            t, m = order[i], i % 2
            power = last_ref[...] if t == EARLY else held[t]
            pltpu.matmul_acc_lhs(accs[i % 4], power, load_staged_rhs=0 if i < 2 else None)

        def collect(i):
            part_ref[order[i]] = pltpu.matmul_pop(accs[i % 4])[:, :PACK]

        for i in range(FRAMES_HERE):
            if i == 1:
                for load in loads[:FIRST_PART]:
                    load.wait()
            if i == 1 + FIRST_PART:
                for load in loads[FIRST_PART:]:
                    load.wait()
            multiply(i)
            if i >= 2:
                collect(i - 2)
        collect(FRAMES_HERE - 2)
        collect(FRAMES_HERE - 1)

    pl.run_scoped(body, *[pltpu.ACC(m)((BINS, TILE), F32) for m in (0, 1, 0, 1)])
    for d in range(N_TM):
        sums = []
        for at in (d * 16, BINS // 2 + d * 16):
            whole = part_ref[0, at:at + 16] * time2_ref[0:1, :]
            for t in range(1, FRAMES_HERE):
                whole = whole + part_ref[t, at:at + 16] * time2_ref[t:t + 1, :]
            sums.append(whole + pltpu.roll(whole, RANK, 1))
        send_ref[d] = jnp.where(lane_is_low((16, PACK)), *sums)


N_GRAM = RANK // 2 // QUAD


def chan_out_kernel(chan_ref, gram_ref, chan_out_ref):
    packed = chan_ref[...].reshape(CHANS_HERE // 2, PACK)
    gram = side_by_side(gram_of(both_halves(packed)))
    for i in range(N_GRAM):
        gram_ref[i] = gram[i * QUAD:(i + 1) * QUAD]
    turned = packed.T
    chan_out_ref[...] = jnp.concatenate([turned[:RANK], turned[RANK:]], axis=1)


def spread_kernel(got_ref, gram_ref, send_ref):
    me = lax.axis_index(TM)
    total = jnp.sum(got_ref[...], axis=0)
    block = gram_ref[me // (N_TM // N_GRAM)]
    for d in range(N_CHAN):
        for i in range(total.shape[0] // QUAD):
            send_ref[d, i] = total[i * QUAD:(i + 1) * QUAD]
        send_ref[d, total.shape[0] // QUAD] = block


def relay_kernel(got_ref, send_ref):
    for i in range(got_ref.shape[1]):
        total = got_ref[0, i]
        for d in range(1, N_CHAN):
            total = total + got_ref[d, i]
        for d in range(N_TM):
            send_ref[d, i] = total


PIECE = 64


def freq_admm_kernel(got_ref, gram_time_ref, start_ref, part_ref, send_ref, new_ref,
                     gram_chan_ref, product_ref, packed_ref):
    rows = BINS // 2 // N_TM
    blocks = rows // QUAD
    for d in range(N_TM):
        for i in range(blocks):
            at = d * rows + i * QUAD
            product_ref[at:at + QUAD, :] = got_ref[d, i]
    for i in range(N_GRAM):
        packed_ref[i * QUAD:(i + 1) * QUAD, :] = got_ref[i * (N_TM // N_GRAM), blocks]
    product = product_ref[...]
    gram = both_halves(packed_ref[...])
    gram_chan_ref[...] = gram
    penalty, inverse = inverse_of(gram * gram_time_ref[...])
    new = admm(product * SCALE, start_ref[...], penalty, inverse)
    new_ref[...] = new
    sums = [jnp.zeros((8, PACK), F32)] * FRAMES_HERE
    half = BINS // 2
    for at in range(0, half, PIECE):
        twice = both_halves(new_ref[at:at + PIECE, :])
        for t in range(FRAMES_HERE):
            for first, side in ((at, twice[:PIECE]), (half + at, twice[PIECE:])):
                piece = part_ref[t, first:first + PIECE] * side
                sums[t] += jnp.sum(piece.reshape(PIECE // 8, 8, PACK), axis=0)
    product = jnp.concatenate([jnp.sum(s, axis=0, keepdims=True) for s in sums], axis=0)
    product = side_by_side(product + pltpu.roll(product, RANK, 1))
    send_ref[...] = jnp.broadcast_to(product[None], send_ref.shape)


def freq_out_kernel(freq_ref, gram_chan_ref, inverse_ref, penalty_ref, freq_out_ref, natural):
    half = BINS // 2
    rows = both_halves(freq_ref[...])
    natural[pl.ds(0, half, stride=2), :] = rows[:half]
    natural[pl.ds(1, half, stride=2), :] = rows[half:]
    freq_out_ref[...] = natural[...].T[:RANK]
    penalty, inverse = inverse_of(gram_of(rows) * gram_chan_ref[...])
    inverse_ref[...] = inverse
    penalty_ref[...] = jnp.full(penalty_ref.shape, penalty, F32)


def time_admm_kernel(got_ref, inverse_ref, penalty_ref, start2_ref, out_ref):
    total = both_halves(jnp.sum(got_ref[...], axis=0))
    new = admm(total * SCALE, start2_ref[...], penalty_ref[...], inverse_ref[...])
    out_ref[...] = new[:, :RANK]


def shape(*dims, dtype=F32):
    return jax.ShapeDtypeStruct(dims, dtype)


def exchanged(parts, axis):
    return lax.all_to_all(parts, axis, split_axis=0, concat_axis=0, tiled=True)


NEAR = pl.BlockSpec(memory_space=pltpu.VMEM)


def near_call(body, name, outs, args, scratch=(), far=(), outside=(), flops=0, others=(),
              kinds_of_others=()):
    def kind(i, o):
        if i in far:
            return o
        return (pltpu.HBM if i in outside else pltpu.VMEM)(o.shape, o.dtype)

    args = [pltpu.with_memory_space_constraint(a, pltpu.VMEM) for a in args]
    args += [pltpu.with_memory_space_constraint(a, pltpu.HBM) for a in others]
    size = sum(a.size * a.dtype.itemsize for a in list(args) + list(outs))
    away = pl.BlockSpec(memory_space=pltpu.HBM)
    return pl.pallas_call(
        body,
        in_specs=[NEAR] * (len(args) - len(others)) + list(kinds_of_others),
        out_specs=tuple(away if i in outside else NEAR for i in range(len(outs))),
        out_shape=tuple(kind(i, o) for i, o in enumerate(outs)),
        scratch_shapes=list(scratch),
        compiler_params=pltpu.CompilerParams(vmem_limit_bytes=32 * 1024 * 1024),
        cost_estimate=pl.CostEstimate(flops=flops, bytes_accessed=size, transcendentals=0),
        name=name,
    )(*args)


def local(samples, start_chan, start_freq, start_time):
    even_table, odd_table = (
        pltpu.with_memory_space_constraint(jnp.asarray(t), pltpu.VMEM) for t in half_tables())
    window = jnp.asarray(window_row())
    flag = pltpu.SemaphoreType.DMA
    outside = pl.BlockSpec(memory_space=pltpu.HBM)
    (head,) = near_call(head_kernel, "head", (shape(CHANS_HERE, HALF, dtype=BF16),), (),
                        [flag(())], others=(samples,), kinds_of_others=[outside])
    route = [(i, i - 1) for i in range(1, N_TM)]
    following = lax.ppermute(head, TM, route)
    natural = [pltpu.VMEM((BINS, PACK), F32)]

    def fixed(*dims):
        return pl.BlockSpec(dims, lambda t: (0,) * len(dims))

    power, early_sum, freq_rows, time2 = pl.pallas_call(
        early_kernel,
        grid=(EARLY,),
        in_specs=[pl.BlockSpec((CHANS_HERE, HALF), lambda t: (0, t)),
                  pl.BlockSpec((CHANS_HERE, HALF), lambda t: (0, t + 1)),
                  fixed(RANK, BINS), fixed(FRAMES_HERE, RANK), fixed(1, HALF),
                  NEAR, NEAR],
        out_specs=[pl.BlockSpec((1, BINS, CHANS_HERE), lambda t: (t, 0, 0)),
                   fixed(PACK, CHANS_HERE), fixed(PACK, BINS), fixed(FRAMES_HERE, PACK)],
        out_shape=(shape(EARLY, BINS, CHANS_HERE, dtype=BF16), shape(PACK, CHANS_HERE),
                   shape(PACK, BINS, dtype=BF16), shape(FRAMES_HERE, PACK)),
        scratch_shapes=natural,
        cost_estimate=pl.CostEstimate(flops=2500000000, bytes_accessed=8000000,
                                      transcendentals=0),
        name="early",
    )(samples, samples, start_freq.T, start_time, window, even_table, odd_table)
    power_last, to_chan = near_call(
        last_kernel, "last", (shape(BINS, CHANS_HERE, dtype=BF16), shape(N_TM, 3, QUAD, PACK)),
        (following, even_table, odd_table),
        [pltpu.VMEM((CHANS_HERE, HALF), BF16), pltpu.VMEM((1, HALF), F32),
         pltpu.VMEM((PACK, BINS), BF16), pltpu.VMEM((FRAMES_HERE, PACK), F32),
         pltpu.VMEM((PACK, CHANS_HERE), F32), flag((5,))],
        far=(1,), others=(samples, window, freq_rows, time2, early_sum),
        kinds_of_others=[outside] * 5)

    got = exchanged(to_chan, TM)
    gram_freq, freq_packed, chan_packed = near_call(
        start_kernel, "start",
        (shape(RANK, PACK), shape(BINS // 2, PACK), shape(CHANS_HERE // 2, PACK)),
        (start_freq.T, start_chan.T), natural)
    chan_rows, gram_time = near_call(
        chan_kernel, "chan", (shape(N_TM, 8, PACK), shape(RANK, PACK)),
        (got, gram_freq, chan_packed))
    chan_all = exchanged(chan_rows, TM)

    part, to_freq = near_call(
        freq_kernel, "freq", (shape(FRAMES_HERE, BINS, PACK), shape(N_TM, 16, PACK)),
        (chan_all, time2, power_last),
        [pltpu.VMEM((CHANS_HERE, TILE), BF16), pltpu.VMEM((EARLY, BINS, CHANS_HERE), BF16),
         flag((EARLY,))], far=(1,), others=(power,), kinds_of_others=[outside])
    got = exchanged(to_freq, TM)
    gram_part, chan_out = near_call(
        chan_out_kernel, "chan_out", (shape(N_GRAM, QUAD, PACK), shape(RANK, CHANS_HERE)),
        (chan_all,), far=(1,))

    (to_all,) = near_call(spread_kernel, "spread", (shape(N_CHAN, 5, QUAD, PACK),),
                          (got, gram_part))
    got = exchanged(to_all, CHAN)
    (to_tm,) = near_call(relay_kernel, "relay", (shape(N_TM, 5, QUAD, PACK),), (got,))
    got = exchanged(to_tm, TM)
    to_all, freq_all, gram_chan = near_call(
        freq_admm_kernel, "freq_admm",
        (shape(N_CHAN, QUAD, PACK), shape(BINS // 2, PACK), shape(RANK, PACK)),
        (got, gram_time, freq_packed, part),
        [pltpu.VMEM((BINS // 2, PACK), F32), pltpu.VMEM((RANK // 2, PACK), F32)], far=(0,))
    got = exchanged(to_all, CHAN)
    inverse, penalty, freq_out = near_call(
        freq_out_kernel, "freq_out",
        (shape(PACK, PACK), shape(1, PACK), shape(RANK, BINS)), (freq_all, gram_chan),
        natural, far=(2,))
    (factor_time,) = near_call(time_admm_kernel, "time_admm", (shape(FRAMES_HERE, RANK),),
                               (got, inverse, penalty, time2), far=(0,))
    return chan_out.T, freq_out.T, factor_time


def solution(mesh):
    finer = Mesh(mesh.devices.reshape(4, 8, 8, 2), ("chan_0", "chan_1", "tm_0", "tm_1"))
    return jax.shard_map(
        local,
        mesh=finer,
        in_specs=(P(CHAN, TM), P(CHAN, None), P(), P(TM, None)),
        out_specs=(P(CHAN, None), P(), P(TM, None)),
        check_vma=False,
    )
```

```python
import numpy as np
import jax
import jax.numpy as jnp
from jax import lax
from jax.experimental import pallas as pl
from jax.experimental.pallas import tpu as pltpu
from jax.sharding import Mesh
from jax.sharding import PartitionSpec as P

FRAME = 1024
HALF = FRAME // 2
BINS = 512
RANK = 64
ITERS = 5
FRAMES_HERE = 8
QUAD = 4
CHANS_HERE = 256
PACK = 2 * RANK
TM = ("tm_0", "tm_1")
N_TM = 16
CHAN = ("chan_0", "chan_1")
N_CHAN = 32
SCALE = 1.0 / (3.0 * FRAME / 8.0)
F32 = jnp.float32
BF16 = jnp.bfloat16
HIGH = lax.Precision.HIGHEST


def half_tables():
    n = np.arange(HALF)[None, :]
    j = np.arange(BINS // 2)[:, None]
    even = 2.0 * np.pi * ((n * (2 * j)) % FRAME) / FRAME
    odd = 2.0 * np.pi * ((n * (2 * j + 1)) % FRAME) / FRAME
    stack = lambda a: np.concatenate([np.cos(a), np.sin(a)], axis=0)
    return stack(even).astype(BF16), stack(odd).astype(BF16)


def window_row():
    n = np.arange(HALF)[None, :]
    return (0.5 - 0.5 * np.cos(2.0 * np.pi * n / FRAME)).astype(np.float32)


def lane_is_low(shape):
    return lax.broadcasted_iota(jnp.int32, shape, 1) < RANK


def both_halves(x):
    other = pltpu.roll(x, RANK, 1)
    low = lane_is_low(x.shape)
    return jnp.concatenate([jnp.where(low, x, other), jnp.where(low, other, x)], axis=0)


def side_by_side(x):
    m = x.shape[0] // 2
    return jnp.where(lane_is_low((m, PACK)), x[:m], x[m:])


def split(x):
    high = x.astype(BF16)
    return high, (x - high.astype(F32)).astype(BF16)


def high_low(x):
    high = x.astype(BF16).astype(F32)
    return jnp.where(lane_is_low(x.shape), high, x - high).astype(BF16)


def doubled(x):
    return jnp.concatenate([x, x], axis=1)


def times(left, right):
    a, b = split(left)
    c, d = split(right)
    both = jnp.concatenate([c, d], axis=1)
    out = jnp.dot(jnp.concatenate([a, b], axis=1), jnp.concatenate([both, both], axis=0),
                  preferred_element_type=F32)
    return out[:, :PACK] + out[:, PACK:]


def times_small(left, right):
    c, d = split(right)
    both = jnp.concatenate([c, d], axis=1)
    out = jnp.dot(high_low(left), jnp.concatenate([both, both], axis=0),
                  preferred_element_type=F32)
    return out[:, :PACK] + out[:, PACK:]


def gram_of(x):
    return times(x.T[:RANK], x)


def inverse_of(gram):
    row = lax.broadcasted_iota(jnp.int32, gram.shape, 0)
    col = lax.broadcasted_iota(jnp.int32, gram.shape, 1)
    eye = jnp.where((row == col) | (row + RANK == col), 1.0, 0.0).astype(F32)
    penalty = jnp.sum(gram * eye) / PACK
    a = gram * (1.0 / penalty) + eye
    mid = RANK / 2.0 + 1.0
    spread = (RANK / 2.0) / mid
    x = eye * (1.0 / mid)
    s = a * (1.0 / mid)
    for step in range(5):
        factor = (2.0 * eye - s) * (1.0 / (1.0 - spread * spread / 2.0))
        spread = (spread * spread / 2.0) / (1.0 - spread * spread / 2.0)
        if step == 0:
            s, x = times_small(s, factor), factor * (1.0 / mid)
        elif step < 4:
            both = times_small(jnp.concatenate([s, x], axis=0), factor)
            s, x = both[:RANK], both[RANK:]
        else:
            x = times_small(x, factor)
    s = times_small(a, x)
    x = times_small(x, 2.0 * eye - s)
    low = lane_is_low(x.shape)
    return penalty, jnp.concatenate([jnp.where(low, x, 0.0), jnp.where(low, 0.0, x)], axis=0)


def admm(product, previous, penalty, inverse):
    scaled = product * (1.0 / penalty)
    carried = previous
    dual = jnp.zeros_like(previous)
    value = previous
    for _ in range(ITERS):
        target = times(scaled + carried, inverse)
        value = target - dual
        dual = jnp.maximum(-value, 0.0)
        carried = jnp.abs(value)
    return jnp.maximum(value, 0.0)


def stacked(x):
    m = x.shape[1] // 2
    return jnp.concatenate([x[:, :m], x[:, m:]], axis=0)


def start_kernel(freq_ref, chan_ref, gram_ref, freq_packed_ref, chan_packed_ref, natural):
    half = BINS // 2
    natural[...] = doubled(freq_ref[...].T)
    even = natural[pl.ds(0, half, stride=2), :]
    odd = natural[pl.ds(1, half, stride=2), :]
    freq_packed_ref[...] = jnp.where(lane_is_low(even.shape), even, odd)
    gram_ref[...] = gram_of(natural[...])
    chan_packed_ref[...] = stacked(chan_ref[...]).T


def frame_power(first, second, window, even_ref, odd_ref):
    first = first.astype(F32) * window
    second = second.astype(F32)
    second = second - second * window
    total = (first + second).astype(BF16)
    change = (first - second).astype(BF16)
    dims = (((1,), (1,)), ((), ()))
    half = BINS // 2
    out = []
    for table, side in ((even_ref, total), (odd_ref, change)):
        wave = lax.dot_general(table[...], side, dims, preferred_element_type=F32)
        out.append((wave[:half] * wave[:half] + wave[half:] * wave[half:]).astype(BF16))
    return jnp.concatenate(out, axis=0)


def chan_term(rows_ref, power, time_row):
    q = jnp.dot(rows_ref[...], power, preferred_element_type=F32)
    row = lax.broadcasted_iota(jnp.int32, (PACK, PACK), 0)
    col = lax.broadcasted_iota(jnp.int32, (PACK, PACK), 1)
    column = jnp.sum(jnp.where(row == col, time_row, 0.0), axis=1, keepdims=True)
    return q * column


EARLY = FRAMES_HERE - 1


def early_kernel(first_ref, second_ref, freq_ref, time_ref, window_ref, even_ref, odd_ref,
                 power_ref, sum_ref, rows_ref, time2_ref, natural):
    t = pl.program_id(0)

    @pl.when(t == 0)
    def _():
        half = BINS // 2
        time2_ref[...] = doubled(time_ref[...])
        natural[...] = doubled(freq_ref[...].T)
        even = natural[pl.ds(0, half, stride=2), :]
        odd = natural[pl.ds(1, half, stride=2), :]
        rows = high_low(jnp.concatenate([even, odd], axis=0))
        rows_ref[...] = rows.astype(F32).T.astype(BF16)
        sum_ref[...] = jnp.zeros_like(sum_ref)

    power = frame_power(first_ref[...], second_ref[...], window_ref[...], even_ref, odd_ref)
    power_ref[0] = power
    sum_ref[...] += chan_term(rows_ref, power, time2_ref[pl.ds(t, 1), :])


def last_kernel(tail_ref, halo_ref, window_ref, even_ref, odd_ref, rows_ref, time2_ref, sum_ref,
                power_ref, send_ref):
    power = frame_power(tail_ref[...], halo_ref[...], window_ref[...], even_ref, odd_ref)
    power_ref[...] = power
    total = sum_ref[...] + chan_term(rows_ref, power, time2_ref[EARLY:, :])
    packed = stacked(total[:RANK] + total[RANK:]).T
    per = CHANS_HERE // 2 // N_TM
    times = side_by_side(time2_ref[...])
    for d in range(N_TM):
        for i in range(per // QUAD):
            send_ref[d, i] = packed[d * per + i * QUAD:d * per + (i + 1) * QUAD]
        send_ref[d, per // QUAD] = times


def ends_kernel(samples_ref, head_ref, tail_ref, sems):
    loads = [pltpu.make_async_copy(samples_ref.at[:, at:at + HALF], ref, sems.at[i])
             for i, (at, ref) in enumerate(((0, head_ref), (EARLY * HALF, tail_ref)))]
    for load in loads:
        load.start()
    for load in loads:
        load.wait()


def chan_kernel(got_ref, gram_freq_ref, start_ref, send_ref, gram_time_ref):
    me = lax.axis_index(TM)
    per = CHANS_HERE // 2 // N_TM
    blocks = per // QUAD
    total = jnp.concatenate(
        [sum(got_ref[d, i] for d in range(N_TM)) for i in range(blocks)], axis=0)
    times = jnp.concatenate([got_ref[d, blocks] for d in range(N_TM)], axis=0)
    gram_time = gram_of(both_halves(times))
    gram_time_ref[...] = gram_time
    penalty, inverse = inverse_of(gram_time * gram_freq_ref[...])
    start = start_ref[pl.ds(pl.multiple_of(me * per, per), per), :]
    new = admm(total * SCALE, start, penalty, inverse)
    send_ref[...] = jnp.broadcast_to(new[None], send_ref.shape)


FIRST_PART = 3
TILE = 256


def freq_kernel(chan_ref, time2_ref, last_ref, early_ref, part_ref, send_ref, sides, held, sems):
    loads = [pltpu.make_async_copy(early_ref.at[t], held.at[t], sems.at[t])
             for t in range(EARLY)]
    for load in loads:
        load.start()
    side = high_low(both_halves(chan_ref[...].reshape(CHANS_HERE // 2, PACK)))
    sides[...] = jnp.concatenate([side, side], axis=1)
    order = [EARLY] + list(range(EARLY))

    def body(*accs):
        for m in (0, 1):
            pltpu.matmul_push_rhs(sides[...], 0, m)

        def multiply(i):
            t, m = order[i], i % 2
            power = last_ref[...] if t == EARLY else held[t]
            pltpu.matmul_acc_lhs(accs[i % 4], power, load_staged_rhs=0 if i < 2 else None)

        def collect(i):
            part_ref[order[i]] = pltpu.matmul_pop(accs[i % 4])[:, :PACK]

        for i in range(FRAMES_HERE):
            if i == 1:
                for load in loads[:FIRST_PART]:
                    load.wait()
            if i == 1 + FIRST_PART:
                for load in loads[FIRST_PART:]:
                    load.wait()
            multiply(i)
            if i >= 2:
                collect(i - 2)
        collect(FRAMES_HERE - 2)
        collect(FRAMES_HERE - 1)

    pl.run_scoped(body, *[pltpu.ACC(m)((BINS, TILE), F32) for m in (0, 1, 0, 1)])
    for d in range(N_TM):
        sums = []
        for at in (d * 16, BINS // 2 + d * 16):
            whole = part_ref[0, at:at + 16] * time2_ref[0:1, :]
            for t in range(1, FRAMES_HERE):
                whole = whole + part_ref[t, at:at + 16] * time2_ref[t:t + 1, :]
            sums.append(whole + pltpu.roll(whole, RANK, 1))
        send_ref[d] = jnp.where(lane_is_low((16, PACK)), *sums)


N_GRAM = RANK // 2 // QUAD


def chan_out_kernel(chan_ref, gram_ref, chan_out_ref):
    packed = chan_ref[...].reshape(CHANS_HERE // 2, PACK)
    gram = side_by_side(gram_of(both_halves(packed)))
    for i in range(N_GRAM):
        gram_ref[i] = gram[i * QUAD:(i + 1) * QUAD]
    turned = packed.T
    chan_out_ref[...] = jnp.concatenate([turned[:RANK], turned[RANK:]], axis=1)


def spread_kernel(got_ref, gram_ref, send_ref):
    me = lax.axis_index(TM)
    total = jnp.sum(got_ref[...], axis=0)
    block = gram_ref[me // (N_TM // N_GRAM)]
    for d in range(N_CHAN):
        for i in range(total.shape[0] // QUAD):
            send_ref[d, i] = total[i * QUAD:(i + 1) * QUAD]
        send_ref[d, total.shape[0] // QUAD] = block


def relay_kernel(got_ref, send_ref):
    for i in range(got_ref.shape[1]):
        total = got_ref[0, i]
        for d in range(1, N_CHAN):
            total = total + got_ref[d, i]
        for d in range(N_TM):
            send_ref[d, i] = total


PIECE = 64


def freq_admm_kernel(got_ref, gram_time_ref, start_ref, part_ref, send_ref, new_ref,
                     gram_chan_ref, product_ref, packed_ref):
    rows = BINS // 2 // N_TM
    blocks = rows // QUAD
    for d in range(N_TM):
        for i in range(blocks):
            at = d * rows + i * QUAD
            product_ref[at:at + QUAD, :] = got_ref[d, i]
    for i in range(N_GRAM):
        packed_ref[i * QUAD:(i + 1) * QUAD, :] = got_ref[i * (N_TM // N_GRAM), blocks]
    product = product_ref[...]
    gram = both_halves(packed_ref[...])
    gram_chan_ref[...] = gram
    penalty, inverse = inverse_of(gram * gram_time_ref[...])
    new = admm(product * SCALE, start_ref[...], penalty, inverse)
    new_ref[...] = new
    sums = [jnp.zeros((8, PACK), F32)] * FRAMES_HERE
    half = BINS // 2
    for at in range(0, half, PIECE):
        twice = both_halves(new_ref[at:at + PIECE, :])
        for t in range(FRAMES_HERE):
            for first, side in ((at, twice[:PIECE]), (half + at, twice[PIECE:])):
                piece = part_ref[t, first:first + PIECE] * side
                sums[t] += jnp.sum(piece.reshape(PIECE // 8, 8, PACK), axis=0)
    product = jnp.concatenate([jnp.sum(s, axis=0, keepdims=True) for s in sums], axis=0)
    product = side_by_side(product + pltpu.roll(product, RANK, 1))
    send_ref[...] = jnp.broadcast_to(product[None], send_ref.shape)


def freq_out_kernel(freq_ref, gram_chan_ref, inverse_ref, penalty_ref, freq_out_ref, natural):
    half = BINS // 2
    rows = both_halves(freq_ref[...])
    natural[pl.ds(0, half, stride=2), :] = rows[:half]
    natural[pl.ds(1, half, stride=2), :] = rows[half:]
    freq_out_ref[...] = natural[...].T[:RANK]
    penalty, inverse = inverse_of(gram_of(rows) * gram_chan_ref[...])
    inverse_ref[...] = inverse
    penalty_ref[...] = jnp.full(penalty_ref.shape, penalty, F32)


def time_admm_kernel(got_ref, inverse_ref, penalty_ref, start2_ref, out_ref):
    total = both_halves(jnp.sum(got_ref[...], axis=0))
    new = admm(total * SCALE, start2_ref[...], penalty_ref[...], inverse_ref[...])
    out_ref[...] = new[:, :RANK]


def shape(*dims, dtype=F32):
    return jax.ShapeDtypeStruct(dims, dtype)


def exchanged(parts, axis):
    return lax.all_to_all(parts, axis, split_axis=0, concat_axis=0, tiled=True)


NEAR = pl.BlockSpec(memory_space=pltpu.VMEM)


def near_call(body, name, outs, args, scratch=(), far=(), outside=(), flops=0, others=(),
              kinds_of_others=()):
    def kind(i, o):
        if i in far:
            return o
        return (pltpu.HBM if i in outside else pltpu.VMEM)(o.shape, o.dtype)

    args = [pltpu.with_memory_space_constraint(a, pltpu.VMEM) for a in args]
    args += [pltpu.with_memory_space_constraint(a, pltpu.HBM) for a in others]
    size = sum(a.size * a.dtype.itemsize for a in list(args) + list(outs))
    away = pl.BlockSpec(memory_space=pltpu.HBM)
    return pl.pallas_call(
        body,
        in_specs=[NEAR] * (len(args) - len(others)) + list(kinds_of_others),
        out_specs=tuple(away if i in outside else NEAR for i in range(len(outs))),
        out_shape=tuple(kind(i, o) for i, o in enumerate(outs)),
        scratch_shapes=list(scratch),
        compiler_params=pltpu.CompilerParams(vmem_limit_bytes=32 * 1024 * 1024),
        cost_estimate=pl.CostEstimate(flops=flops, bytes_accessed=size, transcendentals=0),
        name=name,
    )(*args)


def local(samples, start_chan, start_freq, start_time):
    even_table, odd_table = (
        pltpu.with_memory_space_constraint(jnp.asarray(t), pltpu.VMEM) for t in half_tables())
    window = pltpu.with_memory_space_constraint(jnp.asarray(window_row()), pltpu.VMEM)
    flag = pltpu.SemaphoreType.DMA
    outside = pl.BlockSpec(memory_space=pltpu.HBM)
    piece = shape(CHANS_HERE, HALF, dtype=BF16)
    head, tail = near_call(ends_kernel, "ends", (piece, piece), (), [flag((2,))],
                           others=(samples,), kinds_of_others=[outside])
    route = [(i, i - 1) for i in range(1, N_TM)]
    following = lax.ppermute(head, TM, route)
    natural = [pltpu.VMEM((BINS, PACK), F32)]

    def fixed(*dims):
        return pl.BlockSpec(dims, lambda t: (0,) * len(dims))

    power, early_sum, freq_rows, time2 = pl.pallas_call(
        early_kernel,
        grid=(EARLY,),
        in_specs=[pl.BlockSpec((CHANS_HERE, HALF), lambda t: (0, t)),
                  pl.BlockSpec((CHANS_HERE, HALF), lambda t: (0, t + 1)),
                  fixed(RANK, BINS), fixed(FRAMES_HERE, RANK), NEAR, NEAR, NEAR],
        out_specs=[pl.BlockSpec((1, BINS, CHANS_HERE), lambda t: (t, 0, 0)), NEAR, NEAR, NEAR],
        out_shape=(shape(EARLY, BINS, CHANS_HERE, dtype=BF16),
                   pltpu.VMEM((PACK, CHANS_HERE), F32), pltpu.VMEM((PACK, BINS), BF16),
                   pltpu.VMEM((FRAMES_HERE, PACK), F32)),
        scratch_shapes=natural,
        cost_estimate=pl.CostEstimate(flops=2500000000, bytes_accessed=8000000,
                                      transcendentals=0),
        name="early",
    )(samples, samples, start_freq.T, start_time, window, even_table, odd_table)
    power_last, to_chan = near_call(
        last_kernel, "last", (shape(BINS, CHANS_HERE, dtype=BF16), shape(N_TM, 3, QUAD, PACK)),
        (tail, following, window, even_table, odd_table, freq_rows, time2, early_sum), far=(1,))

    got = exchanged(to_chan, TM)
    gram_freq, freq_packed, chan_packed = near_call(
        start_kernel, "start",
        (shape(RANK, PACK), shape(BINS // 2, PACK), shape(CHANS_HERE // 2, PACK)),
        (start_freq.T, start_chan.T), natural)
    chan_rows, gram_time = near_call(
        chan_kernel, "chan", (shape(N_TM, 8, PACK), shape(RANK, PACK)),
        (got, gram_freq, chan_packed))
    chan_all = exchanged(chan_rows, TM)

    part, to_freq = near_call(
        freq_kernel, "freq", (shape(FRAMES_HERE, BINS, PACK), shape(N_TM, 16, PACK)),
        (chan_all, time2, power_last),
        [pltpu.VMEM((CHANS_HERE, TILE), BF16), pltpu.VMEM((EARLY, BINS, CHANS_HERE), BF16),
         flag((EARLY,))], far=(1,), others=(power,), kinds_of_others=[outside])
    got = exchanged(to_freq, TM)
    gram_part, chan_out = near_call(
        chan_out_kernel, "chan_out", (shape(N_GRAM, QUAD, PACK), shape(RANK, CHANS_HERE)),
        (chan_all,), far=(1,))

    (to_all,) = near_call(spread_kernel, "spread", (shape(N_CHAN, 5, QUAD, PACK),),
                          (got, gram_part))
    got = exchanged(to_all, CHAN)
    (to_tm,) = near_call(relay_kernel, "relay", (shape(N_TM, 5, QUAD, PACK),), (got,))
    got = exchanged(to_tm, TM)
    to_all, freq_all, gram_chan = near_call(
        freq_admm_kernel, "freq_admm",
        (shape(N_CHAN, QUAD, PACK), shape(BINS // 2, PACK), shape(RANK, PACK)),
        (got, gram_time, freq_packed, part),
        [pltpu.VMEM((BINS // 2, PACK), F32), pltpu.VMEM((RANK // 2, PACK), F32)], far=(0,))
    got = exchanged(to_all, CHAN)
    inverse, penalty, freq_out = near_call(
        freq_out_kernel, "freq_out",
        (shape(PACK, PACK), shape(1, PACK), shape(RANK, BINS)), (freq_all, gram_chan),
        natural, far=(2,))
    (factor_time,) = near_call(time_admm_kernel, "time_admm", (shape(FRAMES_HERE, RANK),),
                               (got, inverse, penalty, time2), far=(0,))
    return chan_out.T, freq_out.T, factor_time


def solution(mesh):
    finer = Mesh(mesh.devices.reshape(4, 8, 8, 2), ("chan_0", "chan_1", "tm_0", "tm_1"))
    return jax.shard_map(
        local,
        mesh=finer,
        in_specs=(P(CHAN, TM), P(CHAN, None), P(), P(TM, None)),
        out_specs=(P(CHAN, None), P(), P(TM, None)),
        check_vma=False,
    )
```

```python
import numpy as np
import jax
import jax.numpy as jnp
from jax import lax
from jax.experimental import pallas as pl
from jax.experimental.pallas import tpu as pltpu
from jax.sharding import Mesh
from jax.sharding import PartitionSpec as P

FRAME = 1024
HALF = FRAME // 2
BINS = 512
RANK = 64
ITERS = 5
FRAMES_HERE = 8
QUAD = 4
CHANS_HERE = 256
PACK = 2 * RANK
TM = ("tm_0", "tm_1")
N_TM = 16
CHAN = ("chan_0", "chan_1")
N_CHAN = 32
SCALE = 1.0 / (3.0 * FRAME / 8.0)
F32 = jnp.float32
BF16 = jnp.bfloat16
HIGH = lax.Precision.HIGHEST


def half_tables():
    n = np.arange(HALF)[None, :]
    j = np.arange(BINS // 2)[:, None]
    even = 2.0 * np.pi * ((n * (2 * j)) % FRAME) / FRAME
    odd = 2.0 * np.pi * ((n * (2 * j + 1)) % FRAME) / FRAME
    stack = lambda a: np.concatenate([np.cos(a), np.sin(a)], axis=0)
    return stack(even).astype(BF16), stack(odd).astype(BF16)


def window_row():
    n = np.arange(HALF)[None, :]
    return (0.5 - 0.5 * np.cos(2.0 * np.pi * n / FRAME)).astype(np.float32)


def lane_is_low(shape):
    return lax.broadcasted_iota(jnp.int32, shape, 1) < RANK


def both_halves(x):
    other = pltpu.roll(x, RANK, 1)
    low = lane_is_low(x.shape)
    return jnp.concatenate([jnp.where(low, x, other), jnp.where(low, other, x)], axis=0)


def side_by_side(x):
    m = x.shape[0] // 2
    return jnp.where(lane_is_low((m, PACK)), x[:m], x[m:])


def split(x):
    high = x.astype(BF16)
    return high, (x - high.astype(F32)).astype(BF16)


def high_low(x):
    high = x.astype(BF16).astype(F32)
    return jnp.where(lane_is_low(x.shape), high, x - high).astype(BF16)


def doubled(x):
    return jnp.concatenate([x, x], axis=1)


def times(left, right):
    a, b = split(left)
    c, d = split(right)
    both = jnp.concatenate([c, d], axis=1)
    out = jnp.dot(jnp.concatenate([a, b], axis=1), jnp.concatenate([both, both], axis=0),
                  preferred_element_type=F32)
    return out[:, :PACK] + out[:, PACK:]


def times_small(left, right):
    c, d = split(right)
    both = jnp.concatenate([c, d], axis=1)
    out = jnp.dot(high_low(left), jnp.concatenate([both, both], axis=0),
                  preferred_element_type=F32)
    return out[:, :PACK] + out[:, PACK:]


def gram_of(x):
    return times(x.T[:RANK], x)


def inverse_of(gram):
    row = lax.broadcasted_iota(jnp.int32, gram.shape, 0)
    col = lax.broadcasted_iota(jnp.int32, gram.shape, 1)
    eye = jnp.where((row == col) | (row + RANK == col), 1.0, 0.0).astype(F32)
    penalty = jnp.sum(gram * eye) / PACK
    a = gram * (1.0 / penalty) + eye
    mid = RANK / 2.0 + 1.0
    spread = (RANK / 2.0) / mid
    x = eye * (1.0 / mid)
    s = a * (1.0 / mid)
    for step in range(5):
        factor = (2.0 * eye - s) * (1.0 / (1.0 - spread * spread / 2.0))
        spread = (spread * spread / 2.0) / (1.0 - spread * spread / 2.0)
        if step == 0:
            s, x = times_small(s, factor), factor * (1.0 / mid)
        elif step < 4:
            both = times_small(jnp.concatenate([s, x], axis=0), factor)
            s, x = both[:RANK], both[RANK:]
        else:
            x = times_small(x, factor)
    s = times_small(a, x)
    x = times_small(x, 2.0 * eye - s)
    low = lane_is_low(x.shape)
    return penalty, jnp.concatenate([jnp.where(low, x, 0.0), jnp.where(low, 0.0, x)], axis=0)


def admm(product, previous, penalty, inverse):
    scaled = product * (1.0 / penalty)
    carried = previous
    dual = jnp.zeros_like(previous)
    value = previous
    for _ in range(ITERS):
        target = times(scaled + carried, inverse)
        value = target - dual
        dual = jnp.maximum(-value, 0.0)
        carried = jnp.abs(value)
    return jnp.maximum(value, 0.0)


def stacked(x):
    m = x.shape[1] // 2
    return jnp.concatenate([x[:, :m], x[:, m:]], axis=0)


def start_kernel(freq_ref, chan_ref, gram_ref, freq_packed_ref, chan_packed_ref, natural):
    half = BINS // 2
    natural[...] = doubled(freq_ref[...].T)
    even = natural[pl.ds(0, half, stride=2), :]
    odd = natural[pl.ds(1, half, stride=2), :]
    freq_packed_ref[...] = jnp.where(lane_is_low(even.shape), even, odd)
    gram_ref[...] = gram_of(natural[...])
    chan_packed_ref[...] = stacked(chan_ref[...]).T


def frame_power(first, second, window, even_ref, odd_ref):
    first = first.astype(F32) * window
    second = second.astype(F32)
    second = second - second * window
    total = (first + second).astype(BF16)
    change = (first - second).astype(BF16)
    dims = (((1,), (1,)), ((), ()))
    half = BINS // 2
    out = []
    for table, side in ((even_ref, total), (odd_ref, change)):
        wave = lax.dot_general(table[...], side, dims, preferred_element_type=F32)
        out.append((wave[:half] * wave[:half] + wave[half:] * wave[half:]).astype(BF16))
    return jnp.concatenate(out, axis=0)


def chan_term(rows_ref, power, time_row):
    q = jnp.dot(rows_ref[...], power, preferred_element_type=F32)
    row = lax.broadcasted_iota(jnp.int32, (PACK, PACK), 0)
    col = lax.broadcasted_iota(jnp.int32, (PACK, PACK), 1)
    column = jnp.sum(jnp.where(row == col, time_row, 0.0), axis=1, keepdims=True)
    return q * column


EARLY = FRAMES_HERE - 1


FAR = 4


def early_kernel(first_ref, second_ref, freq_ref, time_ref, window_ref, even_ref, odd_ref,
                 power_ref, near_ref, sum_ref, rows_ref, time2_ref, natural):
    t = pl.program_id(0)

    @pl.when(t == 0)
    def _():
        half = BINS // 2
        time2_ref[...] = doubled(time_ref[...])
        natural[...] = doubled(freq_ref[...].T)
        even = natural[pl.ds(0, half, stride=2), :]
        odd = natural[pl.ds(1, half, stride=2), :]
        rows = high_low(jnp.concatenate([even, odd], axis=0))
        rows_ref[...] = rows.astype(F32).T.astype(BF16)
        sum_ref[...] = jnp.zeros_like(sum_ref)

    power = frame_power(first_ref[...], second_ref[...], window_ref[...], even_ref, odd_ref)
    power_ref[0] = power
    near_ref[jnp.maximum(t - FAR, 0)] = power
    sum_ref[...] += chan_term(rows_ref, power, time2_ref[pl.ds(t, 1), :])


def last_kernel(tail_ref, halo_ref, window_ref, even_ref, odd_ref, rows_ref, time2_ref, sum_ref,
                power_ref, send_ref):
    power = frame_power(tail_ref[...], halo_ref[...], window_ref[...], even_ref, odd_ref)
    power_ref[...] = power
    total = sum_ref[...] + chan_term(rows_ref, power, time2_ref[EARLY:, :])
    packed = stacked(total[:RANK] + total[RANK:]).T
    per = CHANS_HERE // 2 // N_TM
    times = side_by_side(time2_ref[...])
    for d in range(N_TM):
        for i in range(per // QUAD):
            send_ref[d, i] = packed[d * per + i * QUAD:d * per + (i + 1) * QUAD]
        send_ref[d, per // QUAD] = times


def ends_kernel(samples_ref, head_ref, tail_ref, sems):
    loads = [pltpu.make_async_copy(samples_ref.at[:, at:at + HALF], ref, sems.at[i])
             for i, (at, ref) in enumerate(((0, head_ref), (EARLY * HALF, tail_ref)))]
    for load in loads:
        load.start()
    for load in loads:
        load.wait()


def chan_kernel(got_ref, gram_freq_ref, start_ref, send_ref, gram_time_ref):
    me = lax.axis_index(TM)
    per = CHANS_HERE // 2 // N_TM
    blocks = per // QUAD
    total = jnp.concatenate(
        [sum(got_ref[d, i] for d in range(N_TM)) for i in range(blocks)], axis=0)
    times = jnp.concatenate([got_ref[d, blocks] for d in range(N_TM)], axis=0)
    gram_time = gram_of(both_halves(times))
    gram_time_ref[...] = gram_time
    penalty, inverse = inverse_of(gram_time * gram_freq_ref[...])
    start = start_ref[pl.ds(pl.multiple_of(me * per, per), per), :]
    new = admm(total * SCALE, start, penalty, inverse)
    send_ref[...] = jnp.broadcast_to(new[None], send_ref.shape)


TILE = 256


def freq_kernel(chan_ref, time2_ref, last_ref, near_ref, far_ref, part_ref, send_ref,
                sides, held, sems):
    loads = [pltpu.make_async_copy(far_ref.at[t], held.at[t], sems.at[t]) for t in range(FAR)]
    for load in loads:
        load.start()
    side = high_low(both_halves(chan_ref[...].reshape(CHANS_HERE // 2, PACK)))
    sides[...] = jnp.concatenate([side, side], axis=1)
    order = list(range(FAR, FRAMES_HERE)) + list(range(FAR))

    def body(*accs):
        for m in (0, 1):
            pltpu.matmul_push_rhs(sides[...], 0, m)

        def multiply(i):
            t, m = order[i], i % 2
            power = last_ref[...] if t == EARLY else near_ref[t - FAR] if t >= FAR else held[t]
            pltpu.matmul_acc_lhs(accs[i % 4], power, load_staged_rhs=0 if i < 2 else None)

        def collect(i):
            part_ref[order[i]] = pltpu.matmul_pop(accs[i % 4])[:, :PACK]

        for i in range(FRAMES_HERE):
            if order[i] == 0:
                for load in loads:
                    load.wait()
            multiply(i)
            if i >= 2:
                collect(i - 2)
        collect(FRAMES_HERE - 2)
        collect(FRAMES_HERE - 1)

    pl.run_scoped(body, *[pltpu.ACC(m)((BINS, TILE), F32) for m in (0, 1, 0, 1)])
    for d in range(N_TM):
        sums = []
        for at in (d * 16, BINS // 2 + d * 16):
            whole = part_ref[0, at:at + 16] * time2_ref[0:1, :]
            for t in range(1, FRAMES_HERE):
                whole = whole + part_ref[t, at:at + 16] * time2_ref[t:t + 1, :]
            sums.append(whole + pltpu.roll(whole, RANK, 1))
        send_ref[d] = jnp.where(lane_is_low((16, PACK)), *sums)


N_GRAM = RANK // 2 // QUAD


def chan_out_kernel(chan_ref, gram_ref, chan_out_ref):
    packed = chan_ref[...].reshape(CHANS_HERE // 2, PACK)
    gram = side_by_side(gram_of(both_halves(packed)))
    for i in range(N_GRAM):
        gram_ref[i] = gram[i * QUAD:(i + 1) * QUAD]
    turned = packed.T
    chan_out_ref[...] = jnp.concatenate([turned[:RANK], turned[RANK:]], axis=1)


def spread_kernel(got_ref, gram_ref, send_ref):
    me = lax.axis_index(TM)
    total = jnp.sum(got_ref[...], axis=0)
    block = gram_ref[me // (N_TM // N_GRAM)]
    for d in range(N_CHAN):
        for i in range(total.shape[0] // QUAD):
            send_ref[d, i] = total[i * QUAD:(i + 1) * QUAD]
        send_ref[d, total.shape[0] // QUAD] = block


def relay_kernel(got_ref, send_ref):
    for i in range(got_ref.shape[1]):
        total = got_ref[0, i]
        for d in range(1, N_CHAN):
            total = total + got_ref[d, i]
        for d in range(N_TM):
            send_ref[d, i] = total


PIECE = 64


def freq_admm_kernel(got_ref, gram_time_ref, start_ref, part_ref, send_ref, new_ref,
                     gram_chan_ref, product_ref, packed_ref):
    rows = BINS // 2 // N_TM
    blocks = rows // QUAD
    for d in range(N_TM):
        for i in range(blocks):
            at = d * rows + i * QUAD
            product_ref[at:at + QUAD, :] = got_ref[d, i]
    for i in range(N_GRAM):
        packed_ref[i * QUAD:(i + 1) * QUAD, :] = got_ref[i * (N_TM // N_GRAM), blocks]
    product = product_ref[...]
    gram = both_halves(packed_ref[...])
    gram_chan_ref[...] = gram
    penalty, inverse = inverse_of(gram * gram_time_ref[...])
    new = admm(product * SCALE, start_ref[...], penalty, inverse)
    new_ref[...] = new
    sums = [jnp.zeros((8, PACK), F32)] * FRAMES_HERE
    half = BINS // 2
    for at in range(0, half, PIECE):
        twice = both_halves(new_ref[at:at + PIECE, :])
        for t in range(FRAMES_HERE):
            for first, side in ((at, twice[:PIECE]), (half + at, twice[PIECE:])):
                piece = part_ref[t, first:first + PIECE] * side
                sums[t] += jnp.sum(piece.reshape(PIECE // 8, 8, PACK), axis=0)
    product = jnp.concatenate([jnp.sum(s, axis=0, keepdims=True) for s in sums], axis=0)
    product = side_by_side(product + pltpu.roll(product, RANK, 1))
    send_ref[...] = jnp.broadcast_to(product[None], send_ref.shape)


def freq_out_kernel(freq_ref, gram_chan_ref, inverse_ref, penalty_ref, freq_out_ref, natural):
    half = BINS // 2
    rows = both_halves(freq_ref[...])
    natural[pl.ds(0, half, stride=2), :] = rows[:half]
    natural[pl.ds(1, half, stride=2), :] = rows[half:]
    freq_out_ref[...] = natural[...].T[:RANK]
    penalty, inverse = inverse_of(gram_of(rows) * gram_chan_ref[...])
    inverse_ref[...] = inverse
    penalty_ref[...] = jnp.full(penalty_ref.shape, penalty, F32)


def time_admm_kernel(got_ref, inverse_ref, penalty_ref, start2_ref, out_ref):
    total = both_halves(jnp.sum(got_ref[...], axis=0))
    new = admm(total * SCALE, start2_ref[...], penalty_ref[...], inverse_ref[...])
    out_ref[...] = new[:, :RANK]


def shape(*dims, dtype=F32):
    return jax.ShapeDtypeStruct(dims, dtype)


def exchanged(parts, axis):
    return lax.all_to_all(parts, axis, split_axis=0, concat_axis=0, tiled=True)


NEAR = pl.BlockSpec(memory_space=pltpu.VMEM)


def near_call(body, name, outs, args, scratch=(), far=(), outside=(), flops=0, others=(),
              kinds_of_others=()):
    def kind(i, o):
        if i in far:
            return o
        return (pltpu.HBM if i in outside else pltpu.VMEM)(o.shape, o.dtype)

    args = [pltpu.with_memory_space_constraint(a, pltpu.VMEM) for a in args]
    args += [pltpu.with_memory_space_constraint(a, pltpu.HBM) for a in others]
    size = sum(a.size * a.dtype.itemsize for a in list(args) + list(outs))
    away = pl.BlockSpec(memory_space=pltpu.HBM)
    return pl.pallas_call(
        body,
        in_specs=[NEAR] * (len(args) - len(others)) + list(kinds_of_others),
        out_specs=tuple(away if i in outside else NEAR for i in range(len(outs))),
        out_shape=tuple(kind(i, o) for i, o in enumerate(outs)),
        scratch_shapes=list(scratch),
        compiler_params=pltpu.CompilerParams(vmem_limit_bytes=32 * 1024 * 1024),
        cost_estimate=pl.CostEstimate(flops=flops, bytes_accessed=size, transcendentals=0),
        name=name,
    )(*args)


def local(samples, start_chan, start_freq, start_time):
    even_table, odd_table = (
        pltpu.with_memory_space_constraint(jnp.asarray(t), pltpu.VMEM) for t in half_tables())
    window = pltpu.with_memory_space_constraint(jnp.asarray(window_row()), pltpu.VMEM)
    flag = pltpu.SemaphoreType.DMA
    outside = pl.BlockSpec(memory_space=pltpu.HBM)
    piece = shape(CHANS_HERE, HALF, dtype=BF16)
    head, tail = near_call(ends_kernel, "ends", (piece, piece), (), [flag((2,))],
                           others=(samples,), kinds_of_others=[outside])
    route = [(i, i - 1) for i in range(1, N_TM)]
    following = lax.ppermute(head, TM, route)
    natural = [pltpu.VMEM((BINS, PACK), F32)]

    def fixed(*dims):
        return pl.BlockSpec(dims, lambda t: (0,) * len(dims))

    power, power_near, early_sum, freq_rows, time2 = pl.pallas_call(
        early_kernel,
        grid=(EARLY,),
        in_specs=[pl.BlockSpec((CHANS_HERE, HALF), lambda t: (0, t)),
                  pl.BlockSpec((CHANS_HERE, HALF), lambda t: (0, t + 1)),
                  fixed(RANK, BINS), fixed(FRAMES_HERE, RANK), NEAR, NEAR, NEAR],
        out_specs=[pl.BlockSpec((1, BINS, CHANS_HERE),
                                lambda t: (jnp.minimum(t, FAR), 0, 0))] + [NEAR] * 4,
        out_shape=(shape(FAR + 1, BINS, CHANS_HERE, dtype=BF16),
                   pltpu.VMEM((EARLY - FAR, BINS, CHANS_HERE), BF16),
                   pltpu.VMEM((PACK, CHANS_HERE), F32), pltpu.VMEM((PACK, BINS), BF16),
                   pltpu.VMEM((FRAMES_HERE, PACK), F32)),
        scratch_shapes=natural,
        cost_estimate=pl.CostEstimate(flops=2500000000, bytes_accessed=8000000,
                                      transcendentals=0),
        name="early",
    )(samples, samples, start_freq.T, start_time, window, even_table, odd_table)
    power_last, to_chan = near_call(
        last_kernel, "last", (shape(BINS, CHANS_HERE, dtype=BF16), shape(N_TM, 3, QUAD, PACK)),
        (tail, following, window, even_table, odd_table, freq_rows, time2, early_sum), far=(1,))

    got = exchanged(to_chan, TM)
    gram_freq, freq_packed, chan_packed = near_call(
        start_kernel, "start",
        (shape(RANK, PACK), shape(BINS // 2, PACK), shape(CHANS_HERE // 2, PACK)),
        (start_freq.T, start_chan.T), natural)
    chan_rows, gram_time = near_call(
        chan_kernel, "chan", (shape(N_TM, 8, PACK), shape(RANK, PACK)),
        (got, gram_freq, chan_packed))
    chan_all = exchanged(chan_rows, TM)

    part, to_freq = near_call(
        freq_kernel, "freq", (shape(FRAMES_HERE, BINS, PACK), shape(N_TM, 16, PACK)),
        (chan_all, time2, power_last, power_near),
        [pltpu.VMEM((CHANS_HERE, TILE), BF16), pltpu.VMEM((FAR, BINS, CHANS_HERE), BF16),
         flag((FAR,))], far=(1,), others=(power,), kinds_of_others=[outside])
    got = exchanged(to_freq, TM)
    gram_part, chan_out = near_call(
        chan_out_kernel, "chan_out", (shape(N_GRAM, QUAD, PACK), shape(RANK, CHANS_HERE)),
        (chan_all,), far=(1,))

    (to_all,) = near_call(spread_kernel, "spread", (shape(N_CHAN, 5, QUAD, PACK),),
                          (got, gram_part))
    got = exchanged(to_all, CHAN)
    (to_tm,) = near_call(relay_kernel, "relay", (shape(N_TM, 5, QUAD, PACK),), (got,))
    got = exchanged(to_tm, TM)
    to_all, freq_all, gram_chan = near_call(
        freq_admm_kernel, "freq_admm",
        (shape(N_CHAN, QUAD, PACK), shape(BINS // 2, PACK), shape(RANK, PACK)),
        (got, gram_time, freq_packed, part),
        [pltpu.VMEM((BINS // 2, PACK), F32), pltpu.VMEM((RANK // 2, PACK), F32)], far=(0,))
    got = exchanged(to_all, CHAN)
    inverse, penalty, freq_out = near_call(
        freq_out_kernel, "freq_out",
        (shape(PACK, PACK), shape(1, PACK), shape(RANK, BINS)), (freq_all, gram_chan),
        natural, far=(2,))
    (factor_time,) = near_call(time_admm_kernel, "time_admm", (shape(FRAMES_HERE, RANK),),
                               (got, inverse, penalty, time2), far=(0,))
    return chan_out.T, freq_out.T, factor_time


def solution(mesh):
    finer = Mesh(mesh.devices.reshape(4, 8, 8, 2), ("chan_0", "chan_1", "tm_0", "tm_1"))
    return jax.shard_map(
        local,
        mesh=finer,
        in_specs=(P(CHAN, TM), P(CHAN, None), P(), P(TM, None)),
        out_specs=(P(CHAN, None), P(), P(TM, None)),
        check_vma=False,
    )
```
